32 devices in a mesh: groups: 2 (over x), bus: 16 (over z, y, core).
Axes of the slice: x: 2, y: 2, z: 4, core: 2. Of those that a mesh axis runs over, the one named last changes fastest.
Arguments:
- generation: float32 [512, 32], P('bus', 'groups'), parts along dimension 1, may hold values from 0 to 1
- charging: float32 [32, 512], P('groups', 'bus'), parts along dimension 0, may hold values from -1.5 to 1.5
- flow_dual: float32 [4096, 32], P('bus', 'groups'), parts along dimension 1, may hold values from -3 to 3
- energy_dual: float32 [32, 512], P('groups', 'bus'), parts along dimension 0, may hold values from -1.6 to 1.6
- shift_factors: float32 [4096, 16384], P(None, 'bus'), may hold values from -0.0625 to 0.0625
- load_units: int32 [16384, 32], P('bus', 'groups'), parts along dimension 1, may hold values from 0 to 59
- generator_bus: int32 [512], P('bus'), may hold values from 0 to 16383, as said below
- storage_bus: int32 [512], P('bus'), may hold values from 0 to 16383, as said below
- generator_cost: float32 [512], P('bus'), may hold values from 0.05 to 0.5
- generator_max: float32 [512], P('bus'), may hold values from 1 to 4
- charging_max: float32 [512], replicated, may hold values from 2 to 4
- energy_init: float32 [512], replicated, may hold values from 0.5 to 2
- energy_max: float32 [512], replicated, may hold values from 2.5 to 4
- line_max: float32 [4096], P('bus'), may hold values from 0.5 to 3
Outputs:
- generation_new: float32 [512, 32], P('bus', 'groups'), parts along dimension 1
- charging_new: float32 [32, 512], P('groups', 'bus'), parts along dimension 0
- flow_dual_new: float32 [4096, 32], P('bus', 'groups'), parts along dimension 1
- energy_dual_new: float32 [32, 512], P('groups', 'bus'), parts along dimension 0
The draws below stay inside these ranges and needn't reach their ends.
There are 2 independent parts, one for each index of `groups`. The reference program is written for one: setup_inputs(seed, part) draws one part's arguments, and reference() takes and returns one part's arrays. A program takes and returns all parts, laid end to end along the dimension named above; an argument that names none is the same for every part. Nothing has to cross between parts.
Inputs may be any that keep to these rules, and one draw needn't show every extreme that they name: `generator_bus`: generator g sits at one of the buses g // 32 * 1024 to (g // 32 + 1) * 1024 - 1. `storage_bus`: storage unit k sits at one of the buses k // 32 * 1024 to (k // 32 + 1) * 1024 - 1.
All inputs are finite; a program needn't handle non-finite values.
Results may differ from the reference program's by a relative error of at most 0.00023.
Values sent between devices are 32-bit elements; how exact they have to be, the bound alone decides.
No kernel may reach another device: no remote copies, remote signals or barrier semaphores. Data moves between devices by JAX's collectives and lax.ppermute only.
A program may use at most 64 MiB of HBM per device.

```python
import math
import jax
import jax.numpy as jnp
from jax import lax

B = 16384
L = 4096
GEN_DEV = 32
STOR_DEV = 32
ITERS = 3
H = 16
NG = 512
NS = 512
N_BUS = 16


def draw_generator_bus(key, part):
    block = B // N_BUS
    owner = jnp.arange(NG, dtype=jnp.int32) // GEN_DEV
    offset = jax.random.randint(jax.random.fold_in(key, 11), (NG,), 0, block, dtype=jnp.int32)
    return owner * block + offset


def draw_storage_bus(key, part):
    block = B // N_BUS
    owner = jnp.arange(NS, dtype=jnp.int32) // STOR_DEV
    offset = jax.random.randint(jax.random.fold_in(key, 23), (NS,), 0, block, dtype=jnp.int32)
    return owner * block + offset


def touch_ends(values, rng, low, high):
    longest = values.shape.index(max(values.shape))
    spots = []
    for shift in (0, 1):
        where = [jax.random.randint(jax.random.fold_in(rng, axis), (), 0, length) for axis, length in enumerate(values.shape)]
        where[longest] = (where[longest] + shift) % values.shape[longest]
        spots.append(tuple(where))
    return values.at[spots[0]].set(low).at[spots[1]].set(high)


def spiked(drawn, rng, source, target, parts, factor):
    owner, partner = [(jnp.arange(drawn.shape[axis_at]) // (drawn.shape[axis_at] // parts)).reshape([-1 if axis == axis_at else 1 for axis in range(drawn.ndim)]) for axis_at in (source, target)]
    chosen = jax.random.permutation(rng, parts)[partner]
    strong = (owner == chosen) | (owner == (partner + parts // 2) % parts)
    return jnp.where(strong, factor * drawn, drawn)


def level_of(stream_key, extent, shards, least, largest):
    def one(position, parts):
        heights = jax.random.uniform(jax.random.fold_in(jax.random.fold_in(stream_key, 6), position), (parts,), jnp.float32, least / len(shards), largest / len(shards))
        return jnp.repeat(jnp.exp(heights), extent[position] // parts).reshape((-1,) + (1,) * (len(extent) - position - 1))

    loudness = one(*shards[0])
    for cut in shards[1:]:
        loudness = loudness * one(*cut)
    return loudness


def scatter_about(stream_key, dims, spread, reach, split=(), held_as=jnp.bfloat16):
    factor_of = level_of(stream_key, dims, split, -0.22, 0.18) if split else 1.0
    drawn = jax.random.normal(stream_key, dims, jnp.float32) * spread * factor_of
    return jnp.minimum(jnp.maximum(drawn, -reach), reach).astype(held_as)


def bell_draw_with(own_key, shape, width, limit, shards, heavy, held_as=jnp.bfloat16):
    result = width * jax.random.normal(own_key, shape, jnp.float32)
    if shards:
        result = result * level_of(own_key, shape, shards, -0.22, 0.18)
    return jnp.clip(spiked(result, jax.random.fold_in(own_key, 3), *heavy), -limit, limit).astype(held_as)


def setup_inputs(seed: int = 0, part: int = 0) -> dict:
    key_list = jax.random.split(jax.random.key(seed), 15)
    part_splits = jax.random.split(jax.random.fold_in(key_list[14], part), 15)
    generation = jnp.clip(1.0 * jax.random.uniform(part_splits[0], (NG, H), jnp.float32) ** level_of(part_splits[0], (NG, H), ((0, 16),), -0.2, 0.2), 0.0, 1.0)
    charging = jnp.clip(jax.random.uniform(part_splits[1], (H, NS), jnp.float32, -1.5, 1.5) * level_of(part_splits[1], (H, NS), ((1, 16),), -0.4, 0.0), -1.5, 1.5)
    flow_dual = scatter_about(part_splits[2], (L, H), 0.5, 3.0, ((0, 16),), jnp.float32)
    energy_dual = scatter_about(part_splits[3], (H, NS), 0.2, 1.6, ((1, 16),), jnp.float32)
    shift_factors = bell_draw_with(key_list[4], (L, B), B ** -0.5, 0.0625, ((1, 16),), (1, 0, 16, 2.0), jnp.float32)
    load_units = touch_ends(jax.random.randint(part_splits[5], (B, H), 0, 60), jax.random.fold_in(part_splits[5], 1), 0, 59).astype(jnp.int32)
    generator_bus = draw_generator_bus(jax.random.fold_in(key_list[14], 71), part)
    storage_bus = draw_storage_bus(jax.random.fold_in(key_list[14], 71), part)
    generator_cost = jnp.clip(jnp.exp(math.log(0.5) - 2.3025851 * jax.random.uniform(key_list[8], (NG,), jnp.float32) ** level_of(key_list[8], (NG,), ((0, 16),), -0.2, 0.2)), 0.05, 0.5)
    generator_max = jnp.clip(jnp.exp(math.log(4.0) - 1.3862944 * jax.random.uniform(key_list[9], (NG,), jnp.float32) ** level_of(key_list[9], (NG,), ((0, 16),), -0.2, 0.2)), 1.0, 4.0)
    charging_max = jnp.clip(jax.random.uniform(key_list[10], (NS,), jnp.float32, 2.0, 4.0), 2.0, 4.0)
    energy_init = jnp.clip(jax.random.uniform(key_list[11], (NS,), jnp.float32, 0.5, 2.0), 0.5, 2.0)
    energy_max = jnp.clip(jax.random.uniform(key_list[12], (NS,), jnp.float32, 2.5, 4.0), 2.5, 4.0)
    line_max = jnp.clip(0.5 + 2.5 * jax.random.uniform(key_list[13], (L,), jnp.float32) ** level_of(key_list[13], (L,), ((0, 16),), -0.2, 0.2), 0.5, 3.0)
    return {"generation": generation, "charging": charging, "flow_dual": flow_dual, "energy_dual": energy_dual, "shift_factors": shift_factors, "load_units": load_units, "generator_bus": generator_bus, "storage_bus": storage_bus, "generator_cost": generator_cost, "generator_max": generator_max, "charging_max": charging_max, "energy_init": energy_init, "energy_max": energy_max, "line_max": line_max}


primal_step = 0.5
dual_step = 0.5
energy_step = 0.05
efficiency = 0.95
interval = 0.125
load_unit = 0.05


def injection(gen_part, charge_part, load_units, generator_bus, storage_bus):
    from_generators = jax.ops.segment_sum(gen_part, generator_bus, num_segments=B)
    from_storage = jax.ops.segment_sum(charge_part.T, storage_bus, num_segments=B)
    return from_generators - from_storage - load_units.astype(jnp.float32) * load_unit


def reference(generation, charging, flow_dual, energy_dual, shift_factors, load_units, generator_bus, storage_bus, generator_cost, generator_max, charging_max, energy_init, energy_max, line_max):
    for iteration in range(ITERS):
        prices = jnp.dot(shift_factors.T, flow_dual, precision=lax.Precision.HIGHEST, preferred_element_type=jnp.float32)
        later_sum = jnp.flip(jnp.cumsum(jnp.flip(energy_dual, 0), axis=0), 0)
        gen_step = jnp.clip(generation - primal_step * (generator_cost[:, None] + prices[generator_bus]), 0.0, generator_max[:, None])
        gradient = efficiency * interval * later_sum - prices[storage_bus].T
        charge_step = jnp.clip(charging - primal_step * gradient, -charging_max[None, :], charging_max[None, :])
        gen_bar = 2.0 * gen_step - generation
        charge_bar = 2.0 * charge_step - charging
        injected = injection(gen_bar, charge_bar, load_units, generator_bus, storage_bus)
        line_flows = jnp.dot(shift_factors, injected, precision=lax.Precision.HIGHEST, preferred_element_type=jnp.float32)
        moved = flow_dual + dual_step * line_flows
        flow_dual = moved - dual_step * jnp.clip(moved / dual_step, -line_max[:, None], line_max[:, None])
        energy = energy_init[None, :] + efficiency * interval * jnp.cumsum(charge_bar, axis=0)
        shifted = energy_dual + energy_step * energy
        energy_dual = shifted - energy_step * jnp.clip(shifted / energy_step, 0.0, energy_max[None, :])
        generation = gen_step
        charging = charge_step
    return generation, charging, flow_dual, energy_dual
```

```python
import functools

import jax
import jax.numpy as jnp
from jax import lax
from jax.experimental import pallas as pl
from jax.experimental.pallas import tpu as pltpu
from jax.sharding import PartitionSpec as P

ITERS = 3


primal_step = 0.5
dual_step = 0.5
energy_step = 0.05
efficiency = 0.95
interval = 0.125
load_unit = 0.05
rows_by_cols = (((1,), (0,)), ((), ()))
rows_by_rows = (((1,), (1,)), ((), ()))


def split_halves(values):
    high = values.astype(jnp.bfloat16)
    low = (values - high.astype(jnp.float32)).astype(jnp.bfloat16)
    return high, low


def matmul(left, right, dims):
    return lax.dot_general(left, right, dims, preferred_element_type=jnp.float32)


def clip_dual(shifted, step_size, low_bound, high_bound):
    return shifted - step_size * jnp.clip(shifted / step_size, low_bound, high_bound)


def running_sum(values, reverse):
    count = values.shape[0]
    shift = 1
    while shift < count:
        zeros = jnp.zeros((shift, values.shape[1]), values.dtype)
        if reverse:
            moved = jnp.concatenate([values[shift:], zeros], axis=0)
        else:
            moved = jnp.concatenate([zeros, values[:-shift]], axis=0)
        values = values + moved
        shift *= 2
    return values


def scan_kernel(order, factors, weights, columns, base_flow, *, units):
    high, low = split_halves(factors[...])
    w = weights[...]
    found = matmul(high, w, rows_by_cols) + matmul(low, w, rows_by_cols)
    turned = found.T
    top, bottom = split_halves(turned[:units])
    columns[:units, :] = top
    columns[units:, :] = bottom
    base_flow[...] = load_unit * turned[units:]


def scan_factors(order, factors, weights, units, tile):
    lines, buses = factors.shape
    width = weights.shape[1]
    horizon = width - units
    return pl.pallas_call(
        functools.partial(scan_kernel, units=units),
        grid_spec=pltpu.PrefetchScalarGridSpec(
            num_scalar_prefetch=1,
            grid=(lines // tile,),
            in_specs=[
                pl.BlockSpec((tile, buses), lambda i, order: (i, 0)),
                pl.BlockSpec((buses, width), lambda i, order: (0, 0)),
            ],
            out_specs=[
                pl.BlockSpec((2 * units, tile), lambda i, order: (0, order[i])),
                pl.BlockSpec((horizon, tile), lambda i, order: (0, order[i])),
            ],
        ),
        out_shape=[
            jax.ShapeDtypeStruct((2 * units, lines), jnp.bfloat16),
            jax.ShapeDtypeStruct((horizon, lines), jnp.float32),
        ],
        name="scan_factors",
    )(order, factors, weights)


def unit_kernel(
    columns, base_flow, dual, generation, charging, energy_dual, params,
    new_generation, new_charging, new_energy_dual, flows,
):
    horizon, gens = generation.shape
    units = columns.shape[0] // 2
    dual_high, dual_low = split_halves(dual[...])
    cols = columns[...]
    parts = matmul(jnp.concatenate([dual_high, dual_low], axis=0), cols, rows_by_rows)
    prices = parts[:horizon, :units] + parts[:horizon, units:] + parts[horizon:, :units]
    old = generation[...]
    cost = params[0:1, :]
    ceiling = params[1:2, :]
    charge_limit = params[2:3, :]
    start_energy = params[3:4, :]
    energy_limit = params[4:5, :]
    gen_step = jnp.clip(old - primal_step * (cost + prices[:, :gens]), 0.0, ceiling)
    gen_bar = 2.0 * gen_step - old
    new_generation[...] = gen_step
    duals = energy_dual[...]
    held = charging[...]
    gradient = efficiency * interval * running_sum(duals, True) - prices[:, gens:]
    charge_step = jnp.clip(held - primal_step * gradient, -charge_limit, charge_limit)
    charge_bar = 2.0 * charge_step - held
    new_charging[...] = charge_step
    energy = start_energy + efficiency * interval * running_sum(charge_bar, False)
    new_energy_dual[...] = clip_dual(duals + energy_step * energy, energy_step, 0.0, energy_limit)
    bars_high, bars_low = split_halves(jnp.concatenate([gen_bar, -charge_bar], axis=1))
    bars = jnp.concatenate(
        [
            jnp.concatenate([bars_high, bars_high], axis=1),
            jnp.concatenate([bars_low, jnp.zeros_like(bars_low)], axis=1),
        ],
        axis=0,
    )
    both = matmul(bars, cols, rows_by_cols)
    flows[...] = both[:horizon] + both[horizon:] - base_flow[...]


def step_units(columns, base_flow, dual, generation, charging, energy_dual, params):
    like = lambda a: jax.ShapeDtypeStruct(a.shape, jnp.float32)
    return pl.pallas_call(
        unit_kernel,
        out_shape=[like(generation), like(charging), like(energy_dual), like(base_flow)],
        name="step_units",
    )(columns, base_flow, dual, generation, charging, energy_dual, params)


def exchange(values, bit, count):
    return lax.ppermute(values, "bus", [(i, i ^ bit) for i in range(count)])


def on_device(
    generation,
    charging,
    flow_dual,
    energy_dual,
    shift_factors,
    load_units,
    generator_bus,
    storage_bus,
    generator_cost,
    generator_max,
    charging_max,
    energy_init,
    energy_max,
    line_max,
    *,
    count,
):
    lines, buses = shift_factors.shape
    own_lines, horizon = flow_dual.shape
    stor_local = storage_bus.shape[0]
    own = lax.axis_index("bus")
    near_bits = [bit for bit in (1, 2) if bit < count]
    far_bits = [bit for bit in (1 << k for k in range(2, 30)) if bit < count]
    near = 1 << len(near_bits)
    far = count // near
    own_near = own % near
    own_far = own // near
    block = jnp.arange(count, dtype=jnp.int32)
    relative = (block % near) ^ own_near
    turned = jnp.zeros_like(relative)
    for k in range(len(near_bits)):
        turned = turned + ((relative >> k) & 1) * (near >> (k + 1))
    order = turned * far + block // near

    unit_ids = jnp.concatenate([generator_bus, storage_bus])[None, :] - own * buses
    picks = lax.broadcasted_iota(jnp.int32, (buses, 1), 0) == unit_ids
    weights = jnp.concatenate(
        [picks.astype(jnp.bfloat16), load_units.astype(jnp.bfloat16)], axis=1
    )
    units = unit_ids.shape[1]
    if own_lines % 128 == 0:
        columns, base_flow = scan_factors(order, shift_factors, weights, units, own_lines)
    else:
        tile = min(lines, 512)
        plain = jnp.arange(lines // tile, dtype=jnp.int32)
        place = jnp.zeros_like(order).at[order].set(block)
        columns, base_flow = [
            jnp.take(found.reshape(found.shape[0], count, own_lines), place, axis=1).reshape(
                found.shape
            )
            for found in scan_factors(plain, shift_factors, weights, units, tile)
        ]

    first_slot = own * stor_local
    mine = lambda a: lax.dynamic_slice_in_dim(a, first_slot, stor_local)
    params = jnp.stack(
        [generator_cost, generator_max, mine(charging_max), mine(energy_init), mine(energy_max)]
    )

    def sum_far(values):
        for bit in far_bits:
            values = values + exchange(values, bit, count)
        return values

    def gather_near(values):
        for bit in reversed(near_bits):
            values = jnp.concatenate([values, exchange(values, bit, count)], axis=1)
        return values

    def scatter_near(values):
        for bit in near_bits:
            half = values.shape[1] // 2
            values = values[:, :half] + exchange(values[:, half:], bit, count)
        return values

    start = jnp.concatenate([flow_dual.T, line_max[None, :]], axis=0)
    placed = lax.dynamic_update_slice(
        jnp.zeros((horizon + 1, far * own_lines), jnp.float32), start, (0, own_far * own_lines)
    )
    placed = sum_far(placed)
    dual = placed[:horizon]
    limit = placed[horizon:]
    gen_state = generation.T
    for iteration in range(ITERS):
        gen_state, charging, energy_dual, flows = step_units(
            columns, base_flow, gather_near(dual), gen_state, charging, energy_dual, params
        )
        dual = clip_dual(
            dual + dual_step * sum_far(scatter_near(flows)), dual_step, -limit, limit
        )
    own_dual = lax.dynamic_slice_in_dim(dual, own_far * own_lines, own_lines, axis=1)
    return (gen_state.T, charging, own_dual.T, energy_dual)


def solution(mesh):
    placed = (
        P("bus", "groups"),
        P("groups", "bus"),
        P("bus", "groups"),
        P("groups", "bus"),
        P(None, "bus"),
        P("bus", "groups"),
        P("bus"),
        P("bus"),
        P("bus"),
        P("bus"),
        P(),
        P(),
        P(),
        P("bus"),
    )
    return jax.shard_map(
        functools.partial(on_device, count=mesh.shape["bus"]),
        mesh=mesh,
        in_specs=placed,
        out_specs=(P("bus", "groups"), P("groups", "bus"), P("bus", "groups"), P("groups", "bus")),
        check_vma=False,
    )
```

```python
import functools

import jax
import jax.numpy as jnp
from jax import lax
from jax.experimental import pallas as pl
from jax.experimental.pallas import tpu as pltpu
from jax.sharding import PartitionSpec as P

ITERS = 3

QUAD = 4
primal_step = 0.5
dual_step = 0.5
energy_step = 0.05
efficiency = 0.95
interval = 0.125
load_unit = 0.05
rows_by_cols = (((1,), (0,)), ((), ()))
rows_by_rows = (((1,), (1,)), ((), ()))


def split_halves(values):
    high = values.astype(jnp.bfloat16)
    low = (values - high.astype(jnp.float32)).astype(jnp.bfloat16)
    return high, low


def matmul(left, right, dims):
    return lax.dot_general(left, right, dims, preferred_element_type=jnp.float32)


def clip_dual(shifted, step_size, low_bound, high_bound):
    return shifted - step_size * jnp.clip(shifted / step_size, low_bound, high_bound)


def running_sum(values, reverse):
    count = values.shape[0]
    shift = 1
    while shift < count:
        zeros = jnp.zeros((shift, values.shape[1]), values.dtype)
        if reverse:
            moved = jnp.concatenate([values[shift:], zeros], axis=0)
        else:
            moved = jnp.concatenate([zeros, values[:-shift]], axis=0)
        values = values + moved
        shift *= 2
    return values


def near_array(shape, dtype=jnp.float32):
    return pltpu.VMEM(shape, dtype)


def near(values):
    return pltpu.with_memory_space_constraint(values, pltpu.VMEM)


whole_block = pl.BlockSpec(memory_space=pltpu.VMEM)
grant = pltpu.CompilerParams(vmem_limit_bytes=24 << 20)


def as_column(row):
    width = row.shape[1]
    across = lax.broadcasted_iota(jnp.int32, (width, width), 1)
    down = lax.broadcasted_iota(jnp.int32, (width, width), 0)
    return jnp.sum(jnp.where(across == down, row, 0), axis=1, keepdims=True)


def scan_kernel(generator_bus, storage_bus, loads, factors, *rest, wanted, own_lines, far):
    outs = rest[: len(wanted)]
    stage, arrived = rest[len(wanted) :]
    buses = factors.shape[1]
    own = lax.axis_index("bus")
    member = own % QUAD
    copies = []
    for at, r in enumerate(wanted):
        for z in range(far):
            first = (z * QUAD + (member ^ r)) * own_lines
            index = at * far + z
            copy = pltpu.make_async_copy(
                factors.at[pl.ds(pl.multiple_of(first, own_lines), own_lines)],
                stage.at[pl.ds(index * own_lines, own_lines)],
                arrived.at[index],
            )
            copy.start()
            copies.append(copy)
    ids = jnp.concatenate([as_column(generator_bus[...]), as_column(storage_bus[...])], axis=0)
    ids = ids - own * buses
    spots = lax.broadcasted_iota(jnp.int32, (ids.shape[0], buses), 1)
    picks = (spots == ids).astype(jnp.float32)
    weights = jnp.concatenate([picks, loads[...].astype(jnp.float32)], axis=0).astype(jnp.bfloat16)
    units = ids.shape[0]
    quarter = far * own_lines
    tile = max(own_lines, min(128, quarter))
    per_tile = tile // own_lines
    for at in range(len(wanted)):
        for t in range(quarter // tile):
            first = at * far + t * per_tile
            for copy in copies[first : first + per_tile]:
                copy.wait()
            rows = stage[pl.ds(first * own_lines, tile), :]
            high, low = split_halves(rows)
            found = matmul(weights, high, rows_by_rows) + matmul(weights, low, rows_by_rows)
            outs[at][:units, pl.ds(t * tile, tile)] = found[:units]
            outs[at][units:, pl.ds(t * tile, tile)] = load_unit * found[units:]


def scan_factors(generator_bus, storage_bus, loads, factors, wanted, own_lines, far):
    rows = generator_bus.shape[1] + storage_bus.shape[1] + loads.shape[0]
    copies = len(wanted) * far
    return pl.pallas_call(
        functools.partial(scan_kernel, wanted=wanted, own_lines=own_lines, far=far),
        in_specs=[whole_block, whole_block, whole_block, pl.BlockSpec(memory_space=pl.ANY)],
        out_specs=[whole_block] * len(wanted),
        out_shape=[near_array((rows, far * own_lines))] * len(wanted),
        scratch_shapes=[
            pltpu.VMEM((copies * own_lines, factors.shape[1]), jnp.float32),
            pltpu.SemaphoreType.DMA((copies,)),
        ],
        compiler_params=grant,
        name="scan_factors",
    )(generator_bus, storage_bus, loads, factors)


def place_kernel(generation, charging, energy_dual, cost, ceiling, dual, limit, state, lines):
    own = lax.axis_index("bus")
    rows = jnp.concatenate(
        [generation[...], charging[...], energy_dual[...], cost[...], ceiling[...]], axis=0
    )
    for values, out, slot in ((rows, state, own % QUAD), (None, lines, own // QUAD)):
        if values is None:
            values = jnp.concatenate([dual[...], limit[...]], axis=0)
        width = values.shape[1]
        repeats = out.shape[1] // width
        spread = jnp.concatenate([values] * repeats, axis=1)
        where = lax.broadcasted_iota(jnp.int32, spread.shape, 1) // width
        out[...] = jnp.where(where == slot, spread, 0.0)


def place(generation, charging, energy_dual, cost, ceiling, dual, limit, far):
    horizon, gens = generation.shape
    return pl.pallas_call(
        place_kernel,
        out_specs=[whole_block] * 2,
        out_shape=[
            near_array((3 * horizon + 2, QUAD * gens)),
            near_array((horizon + 1, far * dual.shape[1])),
        ],
        compiler_params=grant,
        name="place",
    )(generation, charging, energy_dual, cost, ceiling, dual, limit)


def local_prices(dual, columns):
    horizon = dual.shape[0]
    units = columns.shape[0] // 2
    stacked = jnp.concatenate(split_halves(dual), axis=0)
    parts = matmul(stacked, columns, rows_by_rows)
    return parts[:horizon, :units] + parts[:horizon, units:] + parts[horizon:, :units]


def gather_kernel(block0, block1, block2, block3, dual, columns, base_flow, prices):
    horizon = base_flow.shape[0]
    units = block0.shape[0] - horizon
    group = units // 2
    member = lax.axis_index("bus") % QUAD
    total = None
    for r, block in enumerate((block0, block1, block2, block3)):
        high, low = split_halves(block[:units, :])
        for kind in range(2):
            first = kind * QUAD * group + (member ^ r) * group
            spot = pl.ds(pl.multiple_of(first, group), group)
            columns[spot, :] = high[kind * group : (kind + 1) * group]
            first = first + QUAD * units
            spot = pl.ds(pl.multiple_of(first, group), group)
            columns[spot, :] = low[kind * group : (kind + 1) * group]
        demand = block[units:, :]
        total = demand if total is None else total + demand
    base_flow[...] = total
    prices[...] = local_prices(dual[:horizon, :], columns[...])


def gather_columns(blocks, dual, horizon):
    rows, quarter = blocks[0].shape
    units = rows - horizon
    return pl.pallas_call(
        gather_kernel,
        in_specs=[whole_block] * 5,
        out_specs=[whole_block] * 3,
        out_shape=[
            near_array((2 * QUAD * units, quarter), jnp.bfloat16),
            near_array((horizon, quarter)),
            near_array((horizon, QUAD * units)),
        ],
        compiler_params=grant,
        name="gather_columns",
    )(*[near(block) for block in blocks], near(dual))


def unit_kernel(prices_a, prices_b, state, bounds, columns, base_flow, new_state, flows):
    horizon = flows.shape[0]
    gens = state.shape[1]
    prices = prices_a[...] + prices_b[...]
    old = state[:horizon, :]
    held = state[horizon : 2 * horizon, :]
    duals = state[2 * horizon : 3 * horizon, :]
    cost = state[3 * horizon : 3 * horizon + 1, :]
    ceiling = state[3 * horizon + 1 : 3 * horizon + 2, :]
    charge_limit = bounds[0:1, :]
    start_energy = bounds[1:2, :]
    energy_limit = bounds[2:3, :]
    gen_step = jnp.clip(old - primal_step * (cost + prices[:, :gens]), 0.0, ceiling)
    gen_bar = 2.0 * gen_step - old
    gradient = efficiency * interval * running_sum(duals, True) - prices[:, gens:]
    charge_step = jnp.clip(held - primal_step * gradient, -charge_limit, charge_limit)
    charge_bar = 2.0 * charge_step - held
    bars_high, bars_low = split_halves(jnp.concatenate([gen_bar, -charge_bar], axis=1))
    bars = jnp.concatenate(
        [
            jnp.concatenate([bars_high, bars_high], axis=1),
            jnp.concatenate([bars_low, jnp.zeros_like(bars_low)], axis=1),
        ],
        axis=0,
    )
    both = matmul(bars, columns[...], rows_by_cols)
    flows[...] = both[:horizon] + both[horizon:] - base_flow[...]
    energy = start_energy + efficiency * interval * running_sum(charge_bar, False)
    new_state[:horizon, :] = gen_step
    new_state[horizon : 2 * horizon, :] = charge_step
    new_state[2 * horizon : 3 * horizon, :] = clip_dual(
        duals + energy_step * energy, energy_step, 0.0, energy_limit
    )
    new_state[3 * horizon :, :] = state[3 * horizon :, :]


def step_units(prices_a, prices_b, state, bounds, columns, base_flow):
    return pl.pallas_call(
        unit_kernel,
        in_specs=[whole_block] * 6,
        out_specs=[whole_block] * 2,
        out_shape=[near_array(state.shape), near_array(base_flow.shape)],
        compiler_params=grant,
        name="step_units",
    )(*[near(a) for a in (prices_a, prices_b, state, bounds, columns, base_flow)])


def moved_dual(dual, limit, flows):
    return clip_dual(dual + dual_step * flows, dual_step, -limit, limit)


def line_kernel(lines, flows_a, flows_b, columns, new_lines, prices):
    horizon = flows_a.shape[0]
    limit = lines[horizon:, :]
    dual = moved_dual(lines[:horizon, :], limit, flows_a[...] + flows_b[...])
    new_lines[:horizon, :] = dual
    new_lines[horizon:, :] = limit
    prices[...] = local_prices(dual, columns[...])


def step_lines(lines, flows_a, flows_b, columns):
    return pl.pallas_call(
        line_kernel,
        in_specs=[whole_block] * 4,
        out_specs=[whole_block] * 2,
        out_shape=[
            near_array(lines.shape),
            near_array((flows_a.shape[0], columns.shape[0] // 2)),
        ],
        compiler_params=grant,
        name="step_lines",
    )(*[near(a) for a in (lines, flows_a, flows_b, columns)])


def on_device(
    generation,
    charging,
    flow_dual,
    energy_dual,
    shift_factors,
    load_units,
    generator_bus,
    storage_bus,
    generator_cost,
    generator_max,
    charging_max,
    energy_init,
    energy_max,
    line_max,
    *,
    count,
):
    own_lines, horizon = flow_dual.shape
    own_units = storage_bus.shape[0]
    far = count // QUAD
    own = lax.axis_index("bus")
    member = own % QUAD
    place_of_quad = own // QUAD
    far_bits = [bit for bit in (1 << k for k in range(2, 30)) if bit < count]

    def exchange(values, bit):
        return lax.ppermute(values, "bus", [(i, i ^ bit) for i in range(count)])

    def half_sum(values, bits):
        for bit in bits[:-1]:
            values = values + exchange(values, bit)
        return values, exchange(values, bits[-1])

    scan = functools.partial(
        scan_factors,
        generator_bus[None, :],
        storage_bus[None, :],
        load_units.T,
        shift_factors,
        own_lines=own_lines,
        far=far,
    )
    (for_diagonal,) = scan(wanted=(3,))
    from_diagonal = exchange(for_diagonal, 3)
    (for_y,) = scan(wanted=(2,))
    from_y = exchange(for_y, 2)
    for_core, kept = scan(wanted=(1, 0))
    from_core = exchange(for_core, 1)

    state, lines = place(
        generation.T,
        charging,
        energy_dual,
        generator_cost[None, :],
        generator_max[None, :],
        flow_dual.T,
        line_max[None, :],
        far,
    )
    lines = sum(half_sum(lines, far_bits))
    state = sum(half_sum(state, (1, 2)))
    bounds = lax.dynamic_slice_in_dim(
        jnp.stack([charging_max, energy_init, energy_max]),
        place_of_quad * QUAD * own_units,
        QUAD * own_units,
        axis=1,
    )

    columns, base_flow, prices = gather_columns(
        (kept, from_core, from_y, from_diagonal), lines, horizon
    )
    for iteration in range(ITERS):
        state, flows = step_units(*half_sum(prices, (1, 2)), state, bounds, columns, base_flow)
        flows_a, flows_b = half_sum(flows, far_bits)
        if iteration < ITERS - 1:
            lines, prices = step_lines(lines, flows_a, flows_b, columns)
    mine = lambda a: lax.dynamic_slice_in_dim(a, place_of_quad * own_lines, own_lines, axis=1)
    own_dual = moved_dual(
        mine(lines[:horizon]), mine(lines[horizon:]), mine(flows_a) + mine(flows_b)
    )
    ends = lax.dynamic_slice_in_dim(state, member * own_units, own_units, axis=1)
    return (
        ends[:horizon].T,
        ends[horizon : 2 * horizon],
        own_dual.T,
        ends[2 * horizon : 3 * horizon],
    )


def solution(mesh):
    placed = (
        P("bus", "groups"),
        P("groups", "bus"),
        P("bus", "groups"),
        P("groups", "bus"),
        P(None, "bus"),
        P("bus", "groups"),
        P("bus"),
        P("bus"),
        P("bus"),
        P("bus"),
        P(),
        P(),
        P(),
        P("bus"),
    )
    return jax.shard_map(
        functools.partial(on_device, count=mesh.shape["bus"]),
        mesh=mesh,
        in_specs=placed,
        out_specs=(P("bus", "groups"), P("groups", "bus"), P("bus", "groups"), P("groups", "bus")),
        check_vma=False,
    )
```

```python
import functools

import jax
import jax.numpy as jnp
from jax import lax
from jax.experimental import pallas as pl
from jax.experimental.pallas import tpu as pltpu
from jax.sharding import PartitionSpec as P


ITERS = 3

QUAD = 4
primal_step = 0.5
dual_step = 0.5
energy_step = 0.05
efficiency = 0.95
interval = 0.125
load_unit = 0.05
rows_by_cols = (((1,), (0,)), ((), ()))
rows_by_rows = (((1,), (1,)), ((), ()))


def split_halves(values):
    high = values.astype(jnp.bfloat16)
    low = (values - high.astype(jnp.float32)).astype(jnp.bfloat16)
    return high, low


def matmul(left, right, dims):
    return lax.dot_general(left, right, dims, preferred_element_type=jnp.float32)


def clip_dual(shifted, step_size, low_bound, high_bound):
    return shifted - step_size * jnp.clip(shifted / step_size, low_bound, high_bound)


def running_sum(values, reverse):
    count = values.shape[0]
    shift = 1
    while shift < count:
        zeros = jnp.zeros((shift, values.shape[1]), values.dtype)
        if reverse:
            moved = jnp.concatenate([values[shift:], zeros], axis=0)
        else:
            moved = jnp.concatenate([zeros, values[:-shift]], axis=0)
        values = values + moved
        shift *= 2
    return values


def near_array(shape, dtype=jnp.float32):
    return pltpu.VMEM(shape, dtype)


def near(values):
    return pltpu.with_memory_space_constraint(values, pltpu.VMEM)


def far_array(values):
    return pltpu.with_memory_space_constraint(values, pltpu.HBM)


whole_block = pl.BlockSpec(memory_space=pltpu.VMEM)
grant = pltpu.CompilerParams(vmem_limit_bytes=24 << 20)


def as_column(row):
    width = row.shape[1]
    across = lax.broadcasted_iota(jnp.int32, (width, width), 1)
    down = lax.broadcasted_iota(jnp.int32, (width, width), 0)
    return jnp.sum(jnp.where(across == down, row, 0), axis=1, keepdims=True)


def scan_kernel(
    generator_bus, storage_bus, loads, factors, after, columns, demand,
    stage, arrived, ids_a, ids_b, counts, small,
    *, wanted, own_lines, far,
):
    buses = factors.shape[1]
    own = lax.axis_index("bus")
    member = own % QUAD
    few = []
    for index, (source, target) in enumerate(
        ((generator_bus, ids_a), (storage_bus, ids_b), (loads, counts))
    ):
        few.append(pltpu.make_async_copy(source, target, small.at[index]))
    copies = []
    for at, r in enumerate(wanted):
        for z in range(far):
            first = (z * QUAD + (member ^ r)) * own_lines
            index = at * far + z
            copies.append(
                pltpu.make_async_copy(
                    factors.at[pl.ds(pl.multiple_of(first, own_lines), own_lines)],
                    stage.at[pl.ds(index * own_lines, own_lines)],
                    arrived.at[index],
                )
            )
    for copy in few + copies:
        copy.start()
    for copy in few:
        copy.wait()
    ids = jnp.concatenate([as_column(ids_a[...]), as_column(ids_b[...])], axis=0)
    ids = ids - own * buses
    spots = lax.broadcasted_iota(jnp.int32, (ids.shape[0], buses), 1)
    picks = (spots == ids).astype(jnp.float32)
    weights = jnp.concatenate([picks, counts[...].astype(jnp.float32)], axis=0)
    weights = weights.astype(jnp.bfloat16)
    units = ids.shape[0]
    quarter = far * own_lines
    tile = max(own_lines, min(512, quarter))
    per_tile = tile // own_lines
    for t in range(len(wanted) * quarter // tile):
        first = t * per_tile
        for copy in copies[first : first + per_tile]:
            copy.wait()
        rows = stage[pl.ds(first * own_lines, tile), :]
        high, low = split_halves(rows)
        found = matmul(weights, high, rows_by_rows) + matmul(weights, low, rows_by_rows)
        at, lane = divmod(t * tile, quarter)
        spot = pl.ds(lane, tile)
        columns[at * units : (at + 1) * units, spot] = found[:units]
        horizon = loads.shape[0]
        demand[at * horizon : (at + 1) * horizon, spot] = load_unit * found[units:]


def scan_factors(generator_bus, storage_bus, loads, factors, after, wanted, own_lines, far):
    units = generator_bus.shape[1] + storage_bus.shape[1]
    copies = len(wanted) * far
    quarter = far * own_lines
    arrays = (generator_bus, storage_bus, loads, factors)
    return pl.pallas_call(
        functools.partial(scan_kernel, wanted=wanted, own_lines=own_lines, far=far),
        in_specs=[pl.BlockSpec(memory_space=pltpu.HBM)] * 4 + [pl.BlockSpec(memory_space=pl.ANY)],
        out_specs=[whole_block] * 2,
        out_shape=[
            near_array((len(wanted) * units, quarter)),
            near_array((len(wanted) * loads.shape[0], quarter)),
        ],
        scratch_shapes=[
            pltpu.VMEM((copies * own_lines, factors.shape[1]), jnp.float32),
            pltpu.SemaphoreType.DMA((copies,)),
            pltpu.VMEM(generator_bus.shape, jnp.int32),
            pltpu.VMEM(storage_bus.shape, jnp.int32),
            pltpu.VMEM(loads.shape, jnp.int32),
            pltpu.SemaphoreType.DMA((3,)),
        ],
        compiler_params=grant,
        name="scan_factors",
    )(*[far_array(a) for a in arrays], after)


def place_kernel(generation, charging, energy_dual, cost, ceiling, dual, limit, state, lines):
    own = lax.axis_index("bus")
    rows = jnp.concatenate(
        [generation[...], charging[...], energy_dual[...], cost[...], ceiling[...]], axis=0
    )
    for values, out, slot in ((rows, state, own % QUAD), (None, lines, own // QUAD)):
        if values is None:
            values = jnp.concatenate([dual[...], limit[...]], axis=0)
        width = values.shape[1]
        repeats = out.shape[1] // width
        spread = jnp.concatenate([values] * repeats, axis=1)
        where = lax.broadcasted_iota(jnp.int32, spread.shape, 1) // width
        out[...] = jnp.where(where == slot, spread, 0.0)


def place(generation, charging, energy_dual, cost, ceiling, dual, limit, far):
    horizon, gens = generation.shape
    return pl.pallas_call(
        place_kernel,
        out_specs=[whole_block] * 2,
        out_shape=[
            near_array((3 * horizon + 2, QUAD * gens)),
            near_array((horizon + 1, far * dual.shape[1])),
        ],
        compiler_params=grant,
        name="place",
    )(generation, charging, energy_dual, cost, ceiling, dual, limit)


def local_prices(dual, columns):
    horizon = dual.shape[0]
    units = columns.shape[0] // 2
    stacked = jnp.concatenate(split_halves(dual), axis=0)
    parts = matmul(stacked, columns, rows_by_rows)
    return parts[:horizon, :units] + parts[:horizon, units:] + parts[horizon:, :units]


def gather_kernel(block0, block1, block2, block3, dual, columns, prices):
    horizon = prices.shape[0]
    units = columns.shape[0] // (2 * QUAD)
    group = units // 2
    member = lax.axis_index("bus") % QUAD
    for r, block in enumerate((block0, block1, block2, block3)):
        high, low = split_halves(block[:units, :])
        for kind in range(2):
            first = kind * QUAD * group + (member ^ r) * group
            spot = pl.ds(pl.multiple_of(first, group), group)
            columns[spot, :] = high[kind * group : (kind + 1) * group]
            first = first + QUAD * units
            spot = pl.ds(pl.multiple_of(first, group), group)
            columns[spot, :] = low[kind * group : (kind + 1) * group]
    prices[...] = local_prices(dual[:horizon, :], columns[...])


def gather_columns(blocks, dual, horizon):
    units, quarter = blocks[3].shape
    return pl.pallas_call(
        gather_kernel,
        in_specs=[whole_block] * 5,
        out_specs=[whole_block] * 2,
        out_shape=[
            near_array((2 * QUAD * units, quarter), jnp.bfloat16),
            near_array((horizon, QUAD * units)),
        ],
        compiler_params=grant,
        name="gather_columns",
    )(*[near(block) for block in blocks], near(dual))


def unit_kernel(
    prices_a, prices_b, state, bounds, columns, base_flow, new_state, flows, *held_flows, order
):
    horizon = flows.shape[0]
    gens = state.shape[1]
    prices = prices_a[...] + prices_b[...]
    old = state[:horizon, :]
    held = state[horizon : 2 * horizon, :]
    duals = state[2 * horizon : 3 * horizon, :]
    cost = state[3 * horizon : 3 * horizon + 1, :]
    ceiling = state[3 * horizon + 1 : 3 * horizon + 2, :]
    charge_limit = bounds[0:1, :]
    start_energy = bounds[1:2, :]
    energy_limit = bounds[2:3, :]
    gen_step = jnp.clip(old - primal_step * (cost + prices[:, :gens]), 0.0, ceiling)
    gen_bar = 2.0 * gen_step - old
    gradient = efficiency * interval * running_sum(duals, True) - prices[:, gens:]
    charge_step = jnp.clip(held - primal_step * gradient, -charge_limit, charge_limit)
    charge_bar = 2.0 * charge_step - held
    bars_high, bars_low = split_halves(jnp.concatenate([gen_bar, -charge_bar], axis=1))
    bars = jnp.concatenate(
        [
            jnp.concatenate([bars_high, bars_high], axis=1),
            jnp.concatenate([bars_low, jnp.zeros_like(bars_low)], axis=1),
        ],
        axis=0,
    )
    both = matmul(bars, columns[...], rows_by_cols)
    target = held_flows[0] if order else flows
    target[...] = both[:horizon] + both[horizon:] - base_flow[...]
    if order:
        width = flows.shape[1] // len(order)
        own_far = lax.axis_index("bus") // QUAD
        for at, r in enumerate(order):
            first = pl.multiple_of((own_far ^ r) * width, width)
            flows[:, at * width : (at + 1) * width] = target[:, pl.ds(first, width)]
    energy = start_energy + efficiency * interval * running_sum(charge_bar, False)
    new_state[:horizon, :] = gen_step
    new_state[horizon : 2 * horizon, :] = charge_step
    new_state[2 * horizon : 3 * horizon, :] = clip_dual(
        duals + energy_step * energy, energy_step, 0.0, energy_limit
    )
    new_state[3 * horizon :, :] = state[3 * horizon :, :]


def step_units(prices_a, prices_b, state, bounds, columns, base_flow, order=()):
    return pl.pallas_call(
        functools.partial(unit_kernel, order=order),
        in_specs=[whole_block] * 6,
        out_specs=[whole_block] * 2,
        out_shape=[near_array(state.shape), near_array(base_flow.shape)],
        scratch_shapes=[pltpu.VMEM(base_flow.shape, jnp.float32)] if order else [],
        compiler_params=grant,
        name="step_units",
    )(*[near(a) for a in (prices_a, prices_b, state, bounds, columns, base_flow)])


def moved_dual(dual, limit, flows):
    return clip_dual(dual + dual_step * flows, dual_step, -limit, limit)


def line_kernel(lines, flows_a, flows_b, columns, new_lines, prices):
    horizon = flows_a.shape[0]
    limit = lines[horizon:, :]
    dual = moved_dual(lines[:horizon, :], limit, flows_a[...] + flows_b[...])
    new_lines[:horizon, :] = dual
    new_lines[horizon:, :] = limit
    prices[...] = local_prices(dual, columns[...])


def step_lines(lines, flows_a, flows_b, columns):
    return pl.pallas_call(
        line_kernel,
        in_specs=[whole_block] * 4,
        out_specs=[whole_block] * 2,
        out_shape=[
            near_array(lines.shape),
            near_array((flows_a.shape[0], columns.shape[0] // 2)),
        ],
        compiler_params=grant,
        name="step_lines",
    )(*[near(a) for a in (lines, flows_a, flows_b, columns)])


def on_device(
    generation,
    charging,
    flow_dual,
    energy_dual,
    shift_factors,
    load_units,
    generator_bus,
    storage_bus,
    generator_cost,
    generator_max,
    charging_max,
    energy_init,
    energy_max,
    line_max,
    *,
    count,
):
    own_lines, horizon = flow_dual.shape
    own_units = storage_bus.shape[0]
    far = count // QUAD
    own = lax.axis_index("bus")
    member = own % QUAD
    place_of_quad = own // QUAD
    far_bits = [bit for bit in (1 << k for k in range(2, 30)) if bit < count]

    def exchange(values, bit):
        return lax.ppermute(values, "bus", [(i, i ^ bit) for i in range(count)])

    def half_sum(values, bits):
        for bit in bits[:-1]:
            values = values + exchange(values, bit)
        return values, exchange(values, bits[-1])

    scan = functools.partial(
        scan_factors,
        generator_bus[None, :],
        storage_bus[None, :],
        load_units.T,
        shift_factors,
        own_lines=own_lines,
        far=far,
    )
    units = 2 * own_units
    for_diagonal, demand_3 = scan(generator_bus[None, :], wanted=(3,))
    from_diagonal = exchange(for_diagonal, 3)
    state, lines = place(
        generation.T,
        charging,
        energy_dual,
        generator_cost[None, :],
        generator_max[None, :],
        flow_dual.T,
        line_max[None, :],
        far,
    )
    for bit in far_bits:
        lines = lines + exchange(lines, bit)
    for_y, demand_2 = scan(for_diagonal, wanted=(2,))
    from_y = exchange(for_y, 2)
    rest, demand_1_0 = scan(for_y, wanted=(0, 1))
    from_core = exchange(jnp.concatenate([rest[units:], demand_1_0[horizon:], demand_3], axis=0), 1)
    demand_own = demand_1_0[:horizon] + from_core[units : units + horizon]
    demand_other = demand_2 + from_core[units + horizon :]
    base_flow = demand_own + exchange(demand_other, 2)
    state = sum(half_sum(state, (1, 2)))
    bounds = lax.dynamic_slice_in_dim(
        jnp.stack([charging_max, energy_init, energy_max]),
        place_of_quad * QUAD * own_units,
        QUAD * own_units,
        axis=1,
    )

    columns, prices = gather_columns((rest, from_core, from_y, from_diagonal), lines, horizon)
    for _ in range(ITERS - 1):
        state, flows = step_units(*half_sum(prices, (1, 2)), state, bounds, columns, base_flow)
        lines, prices = step_lines(lines, *half_sum(flows, far_bits), columns)
    mine = lambda a: lax.dynamic_slice_in_dim(a, place_of_quad * own_lines, own_lines, axis=1)
    if own_lines % 128 == 0:
        steps = len(far_bits)
        order = tuple(
            sum(((at >> k) & 1) << (steps - 1 - k) for k in range(steps)) for at in range(far)
        )
    else:
        order = ()
    state, flows = step_units(*half_sum(prices, (1, 2)), state, bounds, columns, base_flow, order)
    if order:
        for bit in far_bits:
            half = flows.shape[1] // 2
            flows = flows[:, :half] + exchange(flows[:, half:], bit)
    else:
        flows = mine(sum(half_sum(flows, far_bits)))
    own_dual = moved_dual(mine(lines[:horizon]), mine(lines[horizon:]), flows)
    ends = lax.dynamic_slice_in_dim(state, member * own_units, own_units, axis=1)
    return (
        ends[:horizon].T,
        ends[horizon : 2 * horizon],
        own_dual.T,
        ends[2 * horizon : 3 * horizon],
    )


def solution(mesh):
    placed = (
        P("bus", "groups"),
        P("groups", "bus"),
        P("bus", "groups"),
        P("groups", "bus"),
        P(None, "bus"),
        P("bus", "groups"),
        P("bus"),
        P("bus"),
        P("bus"),
        P("bus"),
        P(),
        P(),
        P(),
        P("bus"),
    )
    count = mesh.shape["bus"]

    def body(*args):
        return on_device(*args, count=count)

    return jax.shard_map(
        body,
        mesh=mesh,
        in_specs=placed,
        out_specs=(P("bus", "groups"), P("groups", "bus"), P("bus", "groups"), P("groups", "bus")),
        check_vma=False,
    )
```

```python
import functools

import jax
import jax.numpy as jnp
from jax import lax
from jax.experimental import pallas as pl
from jax.experimental.pallas import tpu as pltpu
from jax.sharding import PartitionSpec as P


ITERS = 3

QUAD = 4
primal_step = 0.5
dual_step = 0.5
energy_step = 0.05
efficiency = 0.95
interval = 0.125
load_unit = 0.05
rows_by_cols = (((1,), (0,)), ((), ()))
rows_by_rows = (((1,), (1,)), ((), ()))


def split_halves(values):
    high = values.astype(jnp.bfloat16)
    low = (values - high.astype(jnp.float32)).astype(jnp.bfloat16)
    return high, low


def matmul(left, right, dims):
    return lax.dot_general(left, right, dims, preferred_element_type=jnp.float32)


def clip_dual(shifted, step_size, low_bound, high_bound):
    return shifted - step_size * jnp.clip(shifted / step_size, low_bound, high_bound)


def running_sum(values, reverse):
    count = values.shape[0]
    shift = 1
    while shift < count:
        zeros = jnp.zeros((shift, values.shape[1]), values.dtype)
        if reverse:
            moved = jnp.concatenate([values[shift:], zeros], axis=0)
        else:
            moved = jnp.concatenate([zeros, values[:-shift]], axis=0)
        values = values + moved
        shift *= 2
    return values


def near_array(shape, dtype=jnp.float32):
    return pltpu.VMEM(shape, dtype)


def near(values):
    return pltpu.with_memory_space_constraint(values, pltpu.VMEM)


def far_array(values):
    return pltpu.with_memory_space_constraint(values, pltpu.HBM)


whole_block = pl.BlockSpec(memory_space=pltpu.VMEM)
grant = pltpu.CompilerParams(vmem_limit_bytes=24 << 20)


def as_column(row):
    width = row.shape[1]
    across = lax.broadcasted_iota(jnp.int32, (width, width), 1)
    down = lax.broadcasted_iota(jnp.int32, (width, width), 0)
    return jnp.sum(jnp.where(across == down, row, 0), axis=1, keepdims=True)


def build_weights(generator_bus, storage_bus, loads, own):
    buses = loads.shape[1]
    ids = jnp.concatenate([as_column(generator_bus), as_column(storage_bus)], axis=0)
    ids = ids - own * buses
    spots = lax.broadcasted_iota(jnp.int32, (ids.shape[0], buses), 1)
    picks = (spots == ids).astype(jnp.float32)
    rows = jnp.concatenate([picks, loads.astype(jnp.float32)], axis=0)
    return rows.astype(jnp.bfloat16)


def scan_kernel(*refs, wanted, own_lines, far, units, first_call):
    if first_call:
        generator_bus, storage_bus, loads, factors, columns, demand, weights = refs[:7]
        stage, arrived, ids_a, ids_b, counts, small = refs[7:]
    else:
        weights, factors, _, columns, demand, stage, arrived = refs
    own = lax.axis_index("bus")
    member = own % QUAD
    few = []
    if first_call:
        for index, (source, target) in enumerate(
            ((generator_bus, ids_a), (storage_bus, ids_b), (loads, counts))
        ):
            few.append(pltpu.make_async_copy(source, target, small.at[index]))
    copies = []
    for at, r in enumerate(wanted):
        for z in range(far):
            first = (z * QUAD + (member ^ r)) * own_lines
            index = at * far + z
            copies.append(
                pltpu.make_async_copy(
                    factors.at[pl.ds(pl.multiple_of(first, own_lines), own_lines)],
                    stage.at[pl.ds(index * own_lines, own_lines)],
                    arrived.at[index],
                )
            )
    for copy in few + copies:
        copy.start()
    if first_call:
        for copy in few:
            copy.wait()
        weights[...] = build_weights(ids_a[...], ids_b[...], counts[...], own)
    rows_wanted = weights[...]
    horizon = rows_wanted.shape[0] - units
    quarter = far * own_lines
    tile = max(own_lines, min(512, quarter))
    per_tile = tile // own_lines
    for t in range(len(wanted) * quarter // tile):
        first = t * per_tile
        for copy in copies[first : first + per_tile]:
            copy.wait()
        high, low = split_halves(stage[pl.ds(first * own_lines, tile), :])
        found = matmul(rows_wanted, high, rows_by_rows) + matmul(rows_wanted, low, rows_by_rows)
        at, lane = divmod(t * tile, quarter)
        spot = pl.ds(lane, tile)
        columns[at * units : (at + 1) * units, spot] = found[:units]
        demand[at * horizon : (at + 1) * horizon, spot] = load_unit * found[units:]


def scan_factors(
    factors, own_lines, far, units, horizon, wanted, sources=(), weights=None, after=None
):
    copies = len(wanted) * far
    quarter = far * own_lines
    first_call = weights is None
    distant = pl.BlockSpec(memory_space=pltpu.HBM)
    out_shape = [
        near_array((len(wanted) * units, quarter)),
        near_array((len(wanted) * horizon, quarter)),
    ]
    scratch = [
        pltpu.VMEM((copies * own_lines, factors.shape[1]), jnp.float32),
        pltpu.SemaphoreType.DMA((copies,)),
    ]
    if first_call:
        in_specs = [distant] * 4
        arrays = [far_array(a) for a in (*sources, factors)]
        out_shape.append(near_array((units + horizon, factors.shape[1]), jnp.bfloat16))
        scratch += [pltpu.VMEM(a.shape, jnp.int32) for a in sources]
        scratch.append(pltpu.SemaphoreType.DMA((3,)))
    else:
        in_specs = [whole_block, distant, pl.BlockSpec(memory_space=pl.ANY)]
        arrays = [near(weights), far_array(factors), after]
    return pl.pallas_call(
        functools.partial(
            scan_kernel,
            wanted=wanted,
            own_lines=own_lines,
            far=far,
            units=units,
            first_call=first_call,
        ),
        in_specs=in_specs,
        out_specs=[whole_block] * len(out_shape),
        out_shape=out_shape,
        scratch_shapes=scratch,
        compiler_params=grant,
        name="scan_factors",
    )(*arrays)


def fold(rows, width):
    pieces = [rows[first : first + 8, :] for first in range(0, rows.shape[0], 8)]
    per_row = width // rows.shape[1]
    while len(pieces) % per_row:
        pieces.append(jnp.zeros_like(pieces[0]))
    groups = [
        jnp.concatenate(pieces[first : first + per_row], axis=1)
        for first in range(0, len(pieces), per_row)
    ]
    return jnp.concatenate(groups, axis=0)


def unfold(folded, width):
    return jnp.concatenate(
        [
            folded[first : first + 8, lane : lane + width]
            for first in range(0, folded.shape[0], 8)
            for lane in range(0, folded.shape[1], width)
        ],
        axis=0,
    )


def place_kernel(generation, charging, energy_dual, cost, ceiling, dual, limit, state, lines):
    own = lax.axis_index("bus")

    def spread(values, repeats, slot):
        wide = jnp.concatenate([values] * repeats, axis=1)
        where = lax.broadcasted_iota(jnp.int32, wide.shape, 1) // values.shape[1]
        return jnp.where(where == slot, wide, 0.0)

    rows = [generation[...], charging[...], energy_dual[...], cost[...], ceiling[...]]
    count = sum(values.shape[0] for values in rows)
    rows.append(jnp.zeros((-count % 8, generation.shape[1]), jnp.float32))
    rows = jnp.concatenate(rows, axis=0)
    state[...] = fold(spread(rows, QUAD, own % QUAD), state.shape[1])
    own_lines = jnp.concatenate([dual[...], limit[...]], axis=0)
    lines[...] = spread(own_lines, lines.shape[1] // own_lines.shape[1], own // QUAD)


def place(generation, charging, energy_dual, cost, ceiling, dual, limit, far):
    horizon, gens = generation.shape
    quarter = far * dual.shape[1]
    pieces = (3 * horizon + 2 + 7) // 8
    per_row = quarter // (QUAD * gens)
    groups = (pieces + per_row - 1) // per_row
    return pl.pallas_call(
        place_kernel,
        out_specs=[whole_block] * 2,
        out_shape=[near_array((8 * groups, quarter)), near_array((horizon + 1, quarter))],
        compiler_params=grant,
        name="place",
    )(generation, charging, energy_dual, cost, ceiling, dual, limit)


def local_prices(dual, columns):
    horizon = dual.shape[0]
    units = columns.shape[0] // 2
    stacked = jnp.concatenate(split_halves(dual), axis=0)
    parts = matmul(stacked, columns, rows_by_rows)
    return parts[:horizon, :units] + parts[:horizon, units:] + parts[horizon:, :units]


def gather_kernel(block0, block1, block2, block3, dual, columns, prices):
    horizon = prices.shape[0]
    units = columns.shape[0] // (2 * QUAD)
    group = units // 2
    member = lax.axis_index("bus") % QUAD
    for r, block in enumerate((block0, block1, block2, block3)):
        high, low = split_halves(block[:units, :])
        for kind in range(2):
            first = kind * QUAD * group + (member ^ r) * group
            spot = pl.ds(pl.multiple_of(first, group), group)
            columns[spot, :] = high[kind * group : (kind + 1) * group]
            first = first + QUAD * units
            spot = pl.ds(pl.multiple_of(first, group), group)
            columns[spot, :] = low[kind * group : (kind + 1) * group]
    prices[...] = local_prices(dual[:horizon, :], columns[...])


def gather_columns(blocks, dual, horizon):
    units, quarter = blocks[3].shape
    return pl.pallas_call(
        gather_kernel,
        in_specs=[whole_block] * 5,
        out_specs=[whole_block] * 2,
        out_shape=[
            near_array((2 * QUAD * units, quarter), jnp.bfloat16),
            near_array((horizon, QUAD * units)),
        ],
        compiler_params=grant,
        name="gather_columns",
    )(*[near(block) for block in blocks], near(dual))


def unit_kernel(
    prices_a, prices_b, state, bounds, columns, base_flow, new_state, flows, *held_flows, order
):
    horizon = flows.shape[0]
    count, gens = new_state.shape
    prices = prices_a[...] + prices_b[...]
    now = state[...] if state.shape == new_state.shape else unfold(state[...], gens)[:count]
    old = now[:horizon]
    held = now[horizon : 2 * horizon]
    duals = now[2 * horizon : 3 * horizon]
    cost = now[3 * horizon : 3 * horizon + 1]
    ceiling = now[3 * horizon + 1 : 3 * horizon + 2]
    charge_limit = bounds[0:1, :]
    start_energy = bounds[1:2, :]
    energy_limit = bounds[2:3, :]
    gen_step = jnp.clip(old - primal_step * (cost + prices[:, :gens]), 0.0, ceiling)
    gen_bar = 2.0 * gen_step - old
    gradient = efficiency * interval * running_sum(duals, True) - prices[:, gens:]
    charge_step = jnp.clip(held - primal_step * gradient, -charge_limit, charge_limit)
    charge_bar = 2.0 * charge_step - held
    bars_high, bars_low = split_halves(jnp.concatenate([gen_bar, -charge_bar], axis=1))
    bars = jnp.concatenate(
        [
            jnp.concatenate([bars_high, bars_high], axis=1),
            jnp.concatenate([bars_low, jnp.zeros_like(bars_low)], axis=1),
        ],
        axis=0,
    )
    both = matmul(bars, columns[...], rows_by_cols)
    target = held_flows[0] if order else flows
    target[...] = both[:horizon] + both[horizon:] - base_flow[...]
    if order:
        width = flows.shape[1] // len(order)
        own_far = lax.axis_index("bus") // QUAD
        for at, r in enumerate(order):
            first = pl.multiple_of((own_far ^ r) * width, width)
            flows[:, at * width : (at + 1) * width] = target[:, pl.ds(first, width)]
    energy = start_energy + efficiency * interval * running_sum(charge_bar, False)
    new_state[:horizon, :] = gen_step
    new_state[horizon : 2 * horizon, :] = charge_step
    new_state[2 * horizon : 3 * horizon, :] = clip_dual(
        duals + energy_step * energy, energy_step, 0.0, energy_limit
    )
    new_state[3 * horizon :, :] = now[3 * horizon :]


def step_units(prices_a, prices_b, state, bounds, columns, base_flow, order=()):
    return pl.pallas_call(
        functools.partial(unit_kernel, order=order),
        in_specs=[whole_block] * 6,
        out_specs=[whole_block] * 2,
        out_shape=[
            near_array((3 * base_flow.shape[0] + 2, prices_a.shape[1] // 2)),
            near_array(base_flow.shape),
        ],
        scratch_shapes=[pltpu.VMEM(base_flow.shape, jnp.float32)] if order else [],
        compiler_params=grant,
        name="step_units",
    )(*[near(a) for a in (prices_a, prices_b, state, bounds, columns, base_flow)])


def moved_dual(dual, limit, flows):
    return clip_dual(dual + dual_step * flows, dual_step, -limit, limit)


def line_kernel(lines, flows_a, flows_b, columns, new_lines, prices):
    horizon = flows_a.shape[0]
    limit = lines[horizon:, :]
    dual = moved_dual(lines[:horizon, :], limit, flows_a[...] + flows_b[...])
    new_lines[:horizon, :] = dual
    new_lines[horizon:, :] = limit
    prices[...] = local_prices(dual, columns[...])


def step_lines(lines, flows_a, flows_b, columns):
    return pl.pallas_call(
        line_kernel,
        in_specs=[whole_block] * 4,
        out_specs=[whole_block] * 2,
        out_shape=[
            near_array(lines.shape),
            near_array((flows_a.shape[0], columns.shape[0] // 2)),
        ],
        compiler_params=grant,
        name="step_lines",
    )(*[near(a) for a in (lines, flows_a, flows_b, columns)])


def on_device(
    generation,
    charging,
    flow_dual,
    energy_dual,
    shift_factors,
    load_units,
    generator_bus,
    storage_bus,
    generator_cost,
    generator_max,
    charging_max,
    energy_init,
    energy_max,
    line_max,
    *,
    count,
):
    own_lines, horizon = flow_dual.shape
    own_units = storage_bus.shape[0]
    far = count // QUAD
    own = lax.axis_index("bus")
    member = own % QUAD
    place_of_quad = own // QUAD
    far_bits = [bit for bit in (1 << k for k in range(2, 30)) if bit < count]

    def exchange(values, bit):
        return lax.ppermute(values, "bus", [(i, i ^ bit) for i in range(count)])

    def half_sum(values, bits):
        for bit in bits[:-1]:
            values = values + exchange(values, bit)
        return values, exchange(values, bits[-1])

    units = 2 * own_units
    scan = functools.partial(
        scan_factors, shift_factors, own_lines, far, units, horizon
    )
    for_diagonal, demand_3, weights = scan(
        (3,), sources=(generator_bus[None, :], storage_bus[None, :], load_units.T)
    )
    from_diagonal = exchange(for_diagonal, 3)
    state, lines = place(
        generation.T,
        charging,
        energy_dual,
        generator_cost[None, :],
        generator_max[None, :],
        flow_dual.T,
        line_max[None, :],
        far,
    )
    for bit in far_bits:
        lines = lines + exchange(lines, bit)
    for_y, demand_2 = scan((2,), weights=weights, after=for_diagonal)
    from_y = exchange(for_y, 2)
    rest, demand_1_0 = scan((0, 1), weights=weights, after=for_y)
    from_core = exchange(
        jnp.concatenate([rest[units:], demand_1_0[horizon:], demand_3, state], axis=0), 1
    )
    kept = demand_1_0[:horizon] + from_core[units : units + horizon]
    sent = jnp.concatenate([demand_2, state], axis=0) + from_core[units + horizon :]
    from_y_too = exchange(sent, 2)
    base_flow = kept + from_y_too[:horizon]
    state = sent[horizon:] + from_y_too[horizon:]
    bounds = lax.dynamic_slice_in_dim(
        jnp.stack([charging_max, energy_init, energy_max]),
        place_of_quad * QUAD * own_units,
        QUAD * own_units,
        axis=1,
    )

    columns, prices = gather_columns((rest, from_core, from_y, from_diagonal), lines, horizon)
    for _ in range(ITERS - 1):
        state, flows = step_units(*half_sum(prices, (1, 2)), state, bounds, columns, base_flow)
        lines, prices = step_lines(lines, *half_sum(flows, far_bits), columns)
    mine = lambda a: lax.dynamic_slice_in_dim(a, place_of_quad * own_lines, own_lines, axis=1)
    if own_lines % 128 == 0:
        steps = len(far_bits)
        order = tuple(
            sum(((at >> k) & 1) << (steps - 1 - k) for k in range(steps)) for at in range(far)
        )
    else:
        order = ()
    state, flows = step_units(*half_sum(prices, (1, 2)), state, bounds, columns, base_flow, order)
    if order:
        for bit in far_bits:
            half = flows.shape[1] // 2
            flows = flows[:, :half] + exchange(flows[:, half:], bit)
    else:
        flows = mine(sum(half_sum(flows, far_bits)))
    own_dual = moved_dual(mine(lines[:horizon]), mine(lines[horizon:]), flows)
    ends = lax.dynamic_slice_in_dim(state, member * own_units, own_units, axis=1)
    return (
        ends[:horizon].T,
        ends[horizon : 2 * horizon],
        own_dual.T,
        ends[2 * horizon : 3 * horizon],
    )


def solution(mesh):
    placed = (
        P("bus", "groups"),
        P("groups", "bus"),
        P("bus", "groups"),
        P("groups", "bus"),
        P(None, "bus"),
        P("bus", "groups"),
        P("bus"),
        P("bus"),
        P("bus"),
        P("bus"),
        P(),
        P(),
        P(),
        P("bus"),
    )
    count = mesh.shape["bus"]

    def body(*args):
        return on_device(*args, count=count)

    return jax.shard_map(
        body,
        mesh=mesh,
        in_specs=placed,
        out_specs=(P("bus", "groups"), P("groups", "bus"), P("bus", "groups"), P("groups", "bus")),
        check_vma=False,
    )
```

```python
import functools

import jax
import jax.numpy as jnp
from jax import lax
from jax.experimental import pallas as pl
from jax.experimental.pallas import tpu as pltpu
from jax.sharding import PartitionSpec as P


ITERS = 3

QUAD = 4
primal_step = 0.5
dual_step = 0.5
energy_step = 0.05
efficiency = 0.95
interval = 0.125
load_unit = 0.05
rows_by_cols = (((1,), (0,)), ((), ()))
rows_by_rows = (((1,), (1,)), ((), ()))


def split_halves(values):
    high = values.astype(jnp.bfloat16)
    low = (values - high.astype(jnp.float32)).astype(jnp.bfloat16)
    return high, low


def matmul(left, right, dims):
    return lax.dot_general(left, right, dims, preferred_element_type=jnp.float32)


def clip_dual(shifted, step_size, low_bound, high_bound):
    return shifted - step_size * jnp.clip(shifted / step_size, low_bound, high_bound)


def running_sum(values, reverse):
    count = values.shape[0]
    shift = 1
    while shift < count:
        zeros = jnp.zeros((shift, values.shape[1]), values.dtype)
        if reverse:
            moved = jnp.concatenate([values[shift:], zeros], axis=0)
        else:
            moved = jnp.concatenate([zeros, values[:-shift]], axis=0)
        values = values + moved
        shift *= 2
    return values


def near_array(shape, dtype=jnp.float32):
    return pltpu.VMEM(shape, dtype)


def near(values):
    return pltpu.with_memory_space_constraint(values, pltpu.VMEM)


def far_array(values):
    return pltpu.with_memory_space_constraint(values, pltpu.HBM)


whole_block = pl.BlockSpec(memory_space=pltpu.VMEM)
grant = pltpu.CompilerParams(vmem_limit_bytes=24 << 20)


def total(refs):
    values = refs[0][...]
    for ref in refs[1:]:
        values = values + ref[...]
    return values


def as_column(row):
    width = row.shape[1]
    across = lax.broadcasted_iota(jnp.int32, (width, width), 1)
    down = lax.broadcasted_iota(jnp.int32, (width, width), 0)
    return jnp.sum(jnp.where(across == down, row, 0), axis=1, keepdims=True)


def build_weights(generator_bus, storage_bus, loads, own):
    buses = loads.shape[1]
    ids = jnp.concatenate([as_column(generator_bus), as_column(storage_bus)], axis=0)
    ids = ids - own * buses
    spots = lax.broadcasted_iota(jnp.int32, (ids.shape[0], buses), 1)
    picks = (spots == ids).astype(jnp.float32)
    rows = jnp.concatenate([picks, loads.astype(jnp.float32)], axis=0)
    return rows.astype(jnp.bfloat16)


def scan_kernel(*refs, wanted, own_lines, far, units, first_call):
    if first_call:
        generator_bus, storage_bus, loads, factors, columns, demand, weights = refs[:7]
        stage, arrived, ids_a, ids_b, counts, small = refs[7:]
    else:
        weights, factors, _, columns, demand, stage, arrived = refs
    own = lax.axis_index("bus")
    member = own % QUAD
    few = []
    if first_call:
        for index, (source, target) in enumerate(
            ((generator_bus, ids_a), (storage_bus, ids_b), (loads, counts))
        ):
            few.append(pltpu.make_async_copy(source, target, small.at[index]))
    copies = []
    for at, r in enumerate(wanted):
        for z in range(far):
            first = (z * QUAD + (member ^ r)) * own_lines
            index = at * far + z
            copies.append(
                pltpu.make_async_copy(
                    factors.at[pl.ds(pl.multiple_of(first, own_lines), own_lines)],
                    stage.at[pl.ds(index * own_lines, own_lines)],
                    arrived.at[index],
                )
            )
    early = far if first_call else len(copies)
    for copy in few + copies[:early]:
        copy.start()
    for copy in few:
        copy.wait()
    for copy in copies[early:]:
        copy.start()
    if first_call:
        weights[...] = build_weights(ids_a[...], ids_b[...], counts[...], own)
    rows_wanted = weights[...]
    horizon = rows_wanted.shape[0] - units
    quarter = far * own_lines
    tile = max(own_lines, min(512, quarter))
    per_tile = tile // own_lines
    for t in range(len(wanted) * quarter // tile):
        first = t * per_tile
        for copy in copies[first : first + per_tile]:
            copy.wait()
        high, low = split_halves(stage[pl.ds(first * own_lines, tile), :])
        found = matmul(rows_wanted, high, rows_by_rows) + matmul(rows_wanted, low, rows_by_rows)
        at, lane = divmod(t * tile, quarter)
        spot = pl.ds(lane, tile)
        columns[at * units : (at + 1) * units, spot] = found[:units]
        demand[at * horizon : (at + 1) * horizon, spot] = load_unit * found[units:]


def scan_factors(
    factors, own_lines, far, units, horizon, wanted, sources=(), weights=None, after=None
):
    copies = len(wanted) * far
    quarter = far * own_lines
    first_call = weights is None
    distant = pl.BlockSpec(memory_space=pltpu.HBM)
    out_shape = [
        near_array((len(wanted) * units, quarter)),
        near_array((len(wanted) * horizon, quarter)),
    ]
    scratch = [
        pltpu.VMEM((copies * own_lines, factors.shape[1]), jnp.float32),
        pltpu.SemaphoreType.DMA((copies,)),
    ]
    if first_call:
        in_specs = [distant] * 4
        arrays = [far_array(a) for a in (*sources, factors)]
        out_shape.append(near_array((units + horizon, factors.shape[1]), jnp.bfloat16))
        scratch += [pltpu.VMEM(a.shape, jnp.int32) for a in sources]
        scratch.append(pltpu.SemaphoreType.DMA((3,)))
    else:
        in_specs = [whole_block, distant, pl.BlockSpec(memory_space=pl.ANY)]
        arrays = [near(weights), far_array(factors), after]
    return pl.pallas_call(
        functools.partial(
            scan_kernel,
            wanted=wanted,
            own_lines=own_lines,
            far=far,
            units=units,
            first_call=first_call,
        ),
        in_specs=in_specs,
        out_specs=[whole_block] * len(out_shape),
        out_shape=out_shape,
        scratch_shapes=scratch,
        compiler_params=grant,
        name="scan_factors",
    )(*arrays)


def fold(rows, width):
    pieces = [rows[first : first + 8, :] for first in range(0, rows.shape[0], 8)]
    per_row = width // rows.shape[1]
    while len(pieces) % per_row:
        pieces.append(jnp.zeros_like(pieces[0]))
    groups = [
        jnp.concatenate(pieces[first : first + per_row], axis=1)
        for first in range(0, len(pieces), per_row)
    ]
    return jnp.concatenate(groups, axis=0)


def unfold(folded, width):
    return jnp.concatenate(
        [
            folded[first : first + 8, lane : lane + width]
            for first in range(0, folded.shape[0], 8)
            for lane in range(0, folded.shape[1], width)
        ],
        axis=0,
    )


def place_kernel(generation, charging, energy_dual, cost, ceiling, dual, limit, state, lines):
    own = lax.axis_index("bus")

    def spread(values, repeats, slot):
        wide = jnp.concatenate([values] * repeats, axis=1)
        where = lax.broadcasted_iota(jnp.int32, wide.shape, 1) // values.shape[1]
        return jnp.where(where == slot, wide, 0.0)

    rows = [generation[...], charging[...], energy_dual[...], cost[...], ceiling[...]]
    count = sum(values.shape[0] for values in rows)
    rows.append(jnp.zeros((-count % 8, generation.shape[1]), jnp.float32))
    rows = jnp.concatenate(rows, axis=0)
    state[...] = fold(spread(rows, QUAD, own % QUAD), state.shape[1])
    own_lines = jnp.concatenate([dual[...], limit[...]], axis=0)
    lines[...] = spread(own_lines, lines.shape[1] // own_lines.shape[1], own // QUAD)


def place(generation, charging, energy_dual, cost, ceiling, dual, limit, far):
    horizon, gens = generation.shape
    quarter = far * dual.shape[1]
    pieces = (3 * horizon + 2 + 7) // 8
    per_row = quarter // (QUAD * gens)
    groups = (pieces + per_row - 1) // per_row
    return pl.pallas_call(
        place_kernel,
        out_specs=[whole_block] * 2,
        out_shape=[near_array((8 * groups, quarter)), near_array((horizon + 1, quarter))],
        compiler_params=grant,
        name="place",
    )(generation, charging, energy_dual, cost, ceiling, dual, limit)


def local_prices(dual, columns):
    horizon = dual.shape[0]
    units = columns.shape[0] // 2
    stacked = jnp.concatenate(split_halves(dual), axis=0)
    parts = matmul(stacked, columns, rows_by_rows)
    return parts[:horizon, :units] + parts[:horizon, units:] + parts[horizon:, :units]


def gather_kernel(block0, block1, block2, block3, dual, columns, prices):
    horizon = prices.shape[0]
    units = columns.shape[0] // (2 * QUAD)
    group = units // 2
    member = lax.axis_index("bus") % QUAD
    for r, block in enumerate((block0, block1, block2, block3)):
        high, low = split_halves(block[:units, :])
        for kind in range(2):
            first = kind * QUAD * group + (member ^ r) * group
            spot = pl.ds(pl.multiple_of(first, group), group)
            columns[spot, :] = high[kind * group : (kind + 1) * group]
            first = first + QUAD * units
            spot = pl.ds(pl.multiple_of(first, group), group)
            columns[spot, :] = low[kind * group : (kind + 1) * group]
    prices[...] = local_prices(dual[:horizon, :], columns[...])


def gather_columns(blocks, dual, horizon):
    units, quarter = blocks[3].shape
    return pl.pallas_call(
        gather_kernel,
        in_specs=[whole_block] * 5,
        out_specs=[whole_block] * 2,
        out_shape=[
            near_array((2 * QUAD * units, quarter), jnp.bfloat16),
            near_array((horizon, QUAD * units)),
        ],
        compiler_params=grant,
        name="gather_columns",
    )(*[near(block) for block in blocks], near(dual))


def unit_kernel(*refs, shares, order):
    prices_of, (state, bounds, columns, base_flow, new_state, flows, *held_flows) = (
        refs[:shares],
        refs[shares:],
    )
    horizon = flows.shape[0]
    count, gens = new_state.shape
    prices = total(prices_of)
    now = state[...] if state.shape == new_state.shape else unfold(state[...], gens)[:count]
    old = now[:horizon]
    held = now[horizon : 2 * horizon]
    duals = now[2 * horizon : 3 * horizon]
    cost = now[3 * horizon : 3 * horizon + 1]
    ceiling = now[3 * horizon + 1 : 3 * horizon + 2]
    charge_limit = bounds[0:1, :]
    start_energy = bounds[1:2, :]
    energy_limit = bounds[2:3, :]
    gen_step = jnp.clip(old - primal_step * (cost + prices[:, :gens]), 0.0, ceiling)
    gen_bar = 2.0 * gen_step - old
    gradient = efficiency * interval * running_sum(duals, True) - prices[:, gens:]
    charge_step = jnp.clip(held - primal_step * gradient, -charge_limit, charge_limit)
    charge_bar = 2.0 * charge_step - held
    bars_high, bars_low = split_halves(jnp.concatenate([gen_bar, -charge_bar], axis=1))
    bars = jnp.concatenate(
        [
            jnp.concatenate([bars_high, bars_high], axis=1),
            jnp.concatenate([bars_low, jnp.zeros_like(bars_low)], axis=1),
        ],
        axis=0,
    )
    both = matmul(bars, columns[...], rows_by_cols)
    target = held_flows[0] if order else flows
    target[...] = both[:horizon] + both[horizon:] - base_flow[...]
    if order:
        width = flows.shape[1] // len(order)
        own_far = lax.axis_index("bus") // QUAD
        for at, r in enumerate(order):
            first = pl.multiple_of((own_far ^ r) * width, width)
            flows[:, at * width : (at + 1) * width] = target[:, pl.ds(first, width)]
    energy = start_energy + efficiency * interval * running_sum(charge_bar, False)
    new_state[:horizon, :] = gen_step
    new_state[horizon : 2 * horizon, :] = charge_step
    new_state[2 * horizon : 3 * horizon, :] = clip_dual(
        duals + energy_step * energy, energy_step, 0.0, energy_limit
    )
    new_state[3 * horizon :, :] = now[3 * horizon :]


def step_units(prices, state, bounds, columns, base_flow, order=()):
    return pl.pallas_call(
        functools.partial(unit_kernel, shares=len(prices), order=order),
        in_specs=[whole_block] * (len(prices) + 4),
        out_specs=[whole_block] * 2,
        out_shape=[
            near_array((3 * base_flow.shape[0] + 2, prices[0].shape[1] // 2)),
            near_array(base_flow.shape),
        ],
        scratch_shapes=[pltpu.VMEM(base_flow.shape, jnp.float32)] if order else [],
        compiler_params=grant,
        name="step_units",
    )(*[near(a) for a in (*prices, state, bounds, columns, base_flow)])


def moved_dual(dual, limit, flows):
    return clip_dual(dual + dual_step * flows, dual_step, -limit, limit)


def line_kernel(*refs, shares):
    flows_of, (lines, columns, new_lines, prices) = refs[:shares], refs[shares:]
    horizon = prices.shape[0]
    limit = lines[horizon:, :]
    dual = moved_dual(lines[:horizon, :], limit, total(flows_of))
    new_lines[:horizon, :] = dual
    new_lines[horizon:, :] = limit
    prices[...] = local_prices(dual, columns[...])


def step_lines(flows, lines, columns):
    return pl.pallas_call(
        functools.partial(line_kernel, shares=len(flows)),
        in_specs=[whole_block] * (len(flows) + 2),
        out_specs=[whole_block] * 2,
        out_shape=[
            near_array(lines.shape),
            near_array((flows[0].shape[0], columns.shape[0] // 2)),
        ],
        compiler_params=grant,
        name="step_lines",
    )(*[near(a) for a in (*flows, lines, columns)])


def on_device(
    generation,
    charging,
    flow_dual,
    energy_dual,
    shift_factors,
    load_units,
    generator_bus,
    storage_bus,
    generator_cost,
    generator_max,
    charging_max,
    energy_init,
    energy_max,
    line_max,
    *,
    count,
):
    own_lines, horizon = flow_dual.shape
    own_units = storage_bus.shape[0]
    far = count // QUAD
    own = lax.axis_index("bus")
    member = own % QUAD
    place_of_quad = own // QUAD
    far_bits = [bit for bit in (1 << k for k in range(2, 30)) if bit < count]

    def exchange(values, bit):
        return lax.ppermute(values, "bus", [(i, i ^ bit) for i in range(count)])

    def pairs_of(bits):
        return [bits[first : first + 2] for first in range(0, len(bits), 2)]

    def hops(bits):
        found = [0]
        for bit in bits if bits[0] < QUAD else reversed(bits):
            found += [hop + bit for hop in found]
        return found[1:]

    def shares(values, bits):
        for group in pairs_of(bits):
            parts = [values]
            for hop in hops(group):
                parts.append(exchange(values, hop))
            values = sum(parts)
        return parts

    units = 2 * own_units
    scan = functools.partial(
        scan_factors, shift_factors, own_lines, far, units, horizon
    )
    other, demand_3_2, weights = scan(
        (3, 2), sources=(generator_bus[None, :], storage_bus[None, :], load_units.T)
    )
    from_diagonal = exchange(other[:units], 3)
    from_y = exchange(other[units:], 2)
    state, lines = place(
        generation.T,
        charging,
        energy_dual,
        generator_cost[None, :],
        generator_max[None, :],
        flow_dual.T,
        line_max[None, :],
        far,
    )
    lines = sum(shares(lines, far_bits))
    rest, demand_0_1 = scan((0, 1), weights=weights, after=other)
    from_core = exchange(
        jnp.concatenate([rest[units:], demand_0_1[horizon:], demand_3_2[:horizon], state], axis=0),
        1,
    )
    kept = demand_0_1[:horizon] + from_core[units : units + horizon]
    sent = jnp.concatenate([demand_3_2[horizon:], state], axis=0) + from_core[units + horizon :]
    from_y_too = exchange(sent, 2)
    base_flow = kept + from_y_too[:horizon]
    state = sent[horizon:] + from_y_too[horizon:]
    bounds = lax.dynamic_slice_in_dim(
        jnp.stack([charging_max, energy_init, energy_max]),
        place_of_quad * QUAD * own_units,
        QUAD * own_units,
        axis=1,
    )

    columns, prices = gather_columns((rest, from_core, from_y, from_diagonal), lines, horizon)
    for _ in range(ITERS - 1):
        state, flows = step_units(shares(prices, (1, 2)), state, bounds, columns, base_flow)
        lines, prices = step_lines(shares(flows, far_bits), lines, columns)
    mine = lambda a: lax.dynamic_slice_in_dim(a, place_of_quad * own_lines, own_lines, axis=1)
    if own_lines % 128 == 0:
        steps = len(far_bits)
        order = tuple(
            sum(((at >> k) & 1) << (steps - 1 - k) for k in range(steps)) for at in range(far)
        )
    else:
        order = ()
    state, flows = step_units(shares(prices, (1, 2)), state, bounds, columns, base_flow, order)
    if order:
        for group in pairs_of(far_bits):
            width = flows.shape[1] >> len(group)
            kept = flows[:, :width]
            for hop in hops(group):
                part = sum((hop // bit % 2) << k for k, bit in enumerate(reversed(group)))
                kept = kept + exchange(flows[:, part * width : (part + 1) * width], hop)
            flows = kept
    else:
        flows = mine(sum(shares(flows, far_bits)))
    own_dual = moved_dual(mine(lines[:horizon]), mine(lines[horizon:]), flows)
    ends = lax.dynamic_slice_in_dim(state, member * own_units, own_units, axis=1)
    return (
        ends[:horizon].T,
        ends[horizon : 2 * horizon],
        own_dual.T,
        ends[2 * horizon : 3 * horizon],
    )


def solution(mesh):
    placed = (
        P("bus", "groups"),
        P("groups", "bus"),
        P("bus", "groups"),
        P("groups", "bus"),
        P(None, "bus"),
        P("bus", "groups"),
        P("bus"),
        P("bus"),
        P("bus"),
        P("bus"),
        P(),
        P(),
        P(),
        P("bus"),
    )
    count = mesh.shape["bus"]

    def body(*args):
        return on_device(*args, count=count)

    return jax.shard_map(
        body,
        mesh=mesh,
        in_specs=placed,
        out_specs=(P("bus", "groups"), P("groups", "bus"), P("bus", "groups"), P("groups", "bus")),
        check_vma=False,
    )
```

```python
import functools

import jax
import jax.numpy as jnp
from jax import lax
from jax.experimental import pallas as pl
from jax.experimental.pallas import tpu as pltpu
from jax.sharding import PartitionSpec as P


ITERS = 3

QUAD = 4
primal_step = 0.5
dual_step = 0.5
energy_step = 0.05
efficiency = 0.95
interval = 0.125
load_unit = 0.05
rows_by_cols = (((1,), (0,)), ((), ()))
rows_by_rows = (((1,), (1,)), ((), ()))


def split_halves(values):
    high = values.astype(jnp.bfloat16)
    low = (values - high.astype(jnp.float32)).astype(jnp.bfloat16)
    return high, low


def matmul(left, right, dims):
    return lax.dot_general(left, right, dims, preferred_element_type=jnp.float32)


def clip_dual(shifted, step_size, low_bound, high_bound):
    return shifted - step_size * jnp.clip(shifted / step_size, low_bound, high_bound)


def running_sum(values, reverse):
    count = values.shape[0]
    shift = 1
    while shift < count:
        zeros = jnp.zeros((shift, values.shape[1]), values.dtype)
        if reverse:
            moved = jnp.concatenate([values[shift:], zeros], axis=0)
        else:
            moved = jnp.concatenate([zeros, values[:-shift]], axis=0)
        values = values + moved
        shift *= 2
    return values


def near_array(shape, dtype=jnp.float32):
    return pltpu.VMEM(shape, dtype)


def near(values):
    return pltpu.with_memory_space_constraint(values, pltpu.VMEM)


def far_array(values):
    return pltpu.with_memory_space_constraint(values, pltpu.HBM)


whole_block = pl.BlockSpec(memory_space=pltpu.VMEM)
grant = pltpu.CompilerParams(vmem_limit_bytes=24 << 20)


def total(refs):
    values = refs[0][...]
    for ref in refs[1:]:
        values = values + ref[...]
    return values


def as_column(row):
    width = row.shape[1]
    across = lax.broadcasted_iota(jnp.int32, (width, width), 1)
    down = lax.broadcasted_iota(jnp.int32, (width, width), 0)
    return jnp.sum(jnp.where(across == down, row, 0), axis=1, keepdims=True)


def build_weights(generator_bus, storage_bus, loads, own):
    buses = loads.shape[1]
    ids = jnp.concatenate([as_column(generator_bus), as_column(storage_bus)], axis=0)
    ids = ids - own * buses
    spots = lax.broadcasted_iota(jnp.int32, (ids.shape[0], buses), 1)
    picks = (spots == ids).astype(jnp.float32)
    rows = jnp.concatenate([picks, loads.astype(jnp.float32)], axis=0)
    return rows.astype(jnp.bfloat16)


def scan_kernel(*refs, wanted, own_lines, far, units, first_call):
    if first_call:
        generator_bus, storage_bus, loads, factors, columns, demand, weights = refs[:7]
        stage, arrived, ids_a, ids_b, counts, small = refs[7:]
    else:
        weights, factors, _, columns, demand = refs
    own = lax.axis_index("bus")
    member = own % QUAD
    few = []
    if first_call:
        for index, (source, target) in enumerate(
            ((generator_bus, ids_a), (storage_bus, ids_b), (loads, counts))
        ):
            few.append(pltpu.make_async_copy(source, target, small.at[index]))
    blocks = []
    for r in wanted:
        for z in range(far):
            first = (z * QUAD + (member ^ r)) * own_lines
            blocks.append(factors.at[pl.ds(pl.multiple_of(first, own_lines), own_lines)])
    if first_call:
        copies = [
            pltpu.make_async_copy(
                block, stage.at[pl.ds(index * own_lines, own_lines)], arrived.at[index]
            )
            for index, block in enumerate(blocks)
        ]
        for copy in few + copies[:far]:
            copy.start()
        for copy in few:
            copy.wait()
        for copy in copies[far:]:
            copy.start()
        weights[...] = build_weights(ids_a[...], ids_b[...], counts[...], own)
    rows_wanted = weights[...]
    horizon = rows_wanted.shape[0] - units
    quarter = far * own_lines
    tile = max(own_lines, min(512, quarter))
    per_tile = tile // own_lines
    for t in range(len(wanted) * quarter // tile):
        first = t * per_tile
        if first_call:
            for copy in copies[first : first + per_tile]:
                copy.wait()
            rows = stage[pl.ds(first * own_lines, tile), :]
        else:
            rows = jnp.concatenate(
                [block[...] for block in blocks[first : first + per_tile]], axis=0
            )
        high, low = split_halves(rows)
        found = matmul(rows_wanted, high, rows_by_rows) + matmul(rows_wanted, low, rows_by_rows)
        at, lane = divmod(t * tile, quarter)
        spot = pl.ds(lane, tile)
        columns[at * units : (at + 1) * units, spot] = found[:units]
        demand[at * horizon : (at + 1) * horizon, spot] = load_unit * found[units:]


def scan_factors(
    factors, own_lines, far, units, horizon, wanted, sources=(), weights=None, after=None
):
    copies = len(wanted) * far
    quarter = far * own_lines
    first_call = weights is None
    distant = pl.BlockSpec(memory_space=pltpu.HBM)
    out_shape = [
        near_array((len(wanted) * units, quarter)),
        near_array((len(wanted) * horizon, quarter)),
    ]
    scratch = []
    if first_call:
        scratch += [
            pltpu.VMEM((copies * own_lines, factors.shape[1]), jnp.float32),
            pltpu.SemaphoreType.DMA((copies,)),
        ]
        in_specs = [distant] * 4
        arrays = [far_array(a) for a in (*sources, factors)]
        out_shape.append(near_array((units + horizon, factors.shape[1]), jnp.bfloat16))
        scratch += [pltpu.VMEM(a.shape, jnp.int32) for a in sources]
        scratch.append(pltpu.SemaphoreType.DMA((3,)))
    else:
        in_specs = [whole_block, whole_block, pl.BlockSpec(memory_space=pl.ANY)]
        arrays = [near(weights), near(factors), after]
    return pl.pallas_call(
        functools.partial(
            scan_kernel,
            wanted=wanted,
            own_lines=own_lines,
            far=far,
            units=units,
            first_call=first_call,
        ),
        in_specs=in_specs,
        out_specs=[whole_block] * len(out_shape),
        out_shape=out_shape,
        scratch_shapes=scratch,
        compiler_params=grant,
        name="scan_factors",
    )(*arrays)


def fold(rows, width):
    pieces = [rows[first : first + 8, :] for first in range(0, rows.shape[0], 8)]
    per_row = width // rows.shape[1]
    while len(pieces) % per_row:
        pieces.append(jnp.zeros_like(pieces[0]))
    groups = [
        jnp.concatenate(pieces[first : first + per_row], axis=1)
        for first in range(0, len(pieces), per_row)
    ]
    return jnp.concatenate(groups, axis=0)


def unfold(folded, width):
    return jnp.concatenate(
        [
            folded[first : first + 8, lane : lane + width]
            for first in range(0, folded.shape[0], 8)
            for lane in range(0, folded.shape[1], width)
        ],
        axis=0,
    )


def place_kernel(generation, charging, energy_dual, cost, ceiling, dual, limit, state, lines):
    own = lax.axis_index("bus")

    def spread(values, repeats, slot):
        wide = jnp.concatenate([values] * repeats, axis=1)
        where = lax.broadcasted_iota(jnp.int32, wide.shape, 1) // values.shape[1]
        return jnp.where(where == slot, wide, 0.0)

    rows = [generation[...], charging[...], energy_dual[...], cost[...], ceiling[...]]
    count = sum(values.shape[0] for values in rows)
    rows.append(jnp.zeros((-count % 8, generation.shape[1]), jnp.float32))
    rows = jnp.concatenate(rows, axis=0)
    state[...] = fold(spread(rows, QUAD, own % QUAD), state.shape[1])
    own_lines = jnp.concatenate([dual[...], limit[...]], axis=0)
    if lines.shape == own_lines.shape:
        lines[...] = own_lines
    else:
        lines[...] = spread(own_lines, lines.shape[1] // own_lines.shape[1], own // QUAD)


def place(generation, charging, energy_dual, cost, ceiling, dual, limit, far, alone):
    horizon, gens = generation.shape
    quarter = far * dual.shape[1]
    pieces = (3 * horizon + 2 + 7) // 8
    per_row = quarter // (QUAD * gens)
    groups = (pieces + per_row - 1) // per_row
    return pl.pallas_call(
        place_kernel,
        out_specs=[whole_block] * 2,
        out_shape=[
            near_array((8 * groups, quarter)),
            near_array((horizon + 1, dual.shape[1] if alone else quarter)),
        ],
        compiler_params=grant,
        name="place",
    )(generation, charging, energy_dual, cost, ceiling, dual, limit)


def local_prices(dual, columns):
    horizon = dual.shape[0]
    units = columns.shape[0] // 2
    stacked = jnp.concatenate(split_halves(dual), axis=0)
    parts = matmul(stacked, columns, rows_by_rows)
    return parts[:horizon, :units] + parts[:horizon, units:] + parts[horizon:, :units]


def gather_kernel(block0, block1, block2, block3, *refs, hops):
    parts, (lines, columns, prices) = refs[:-3], refs[-3:]
    horizon = prices.shape[0]
    for hop, part in zip(hops, parts):
        if part.shape == lines.shape:
            lines[...] = part[...]
        else:
            width = part.shape[1]
            first = pl.multiple_of((lax.axis_index("bus") // QUAD ^ hop) * width, width)
            lines[:, pl.ds(first, width)] = part[...]
    units = columns.shape[0] // (2 * QUAD)
    group = units // 2
    member = lax.axis_index("bus") % QUAD
    for r, block in enumerate((block0, block1, block2, block3)):
        high, low = split_halves(block[:units, :])
        for kind in range(2):
            first = kind * QUAD * group + (member ^ r) * group
            spot = pl.ds(pl.multiple_of(first, group), group)
            columns[spot, :] = high[kind * group : (kind + 1) * group]
            first = first + QUAD * units
            spot = pl.ds(pl.multiple_of(first, group), group)
            columns[spot, :] = low[kind * group : (kind + 1) * group]
    prices[...] = local_prices(lines[:horizon, :], columns[...])


def gather_columns(blocks, parts, hops, horizon):
    units, quarter = blocks[3].shape
    arrays = [near(a) for a in (*blocks, *parts)]
    return pl.pallas_call(
        functools.partial(gather_kernel, hops=hops),
        in_specs=[whole_block] * len(arrays),
        out_specs=[whole_block] * 3,
        out_shape=[
            near_array((horizon + 1, quarter)),
            near_array((2 * QUAD * units, quarter), jnp.bfloat16),
            near_array((horizon, QUAD * units)),
        ],
        compiler_params=grant,
        name="gather_columns",
    )(*arrays)


def unit_kernel(*refs, shares, order):
    prices_of, (state, bounds, columns, base_flow, new_state, flows, *held_flows) = (
        refs[:shares],
        refs[shares:],
    )
    horizon = flows.shape[0]
    count, gens = new_state.shape
    prices = total(prices_of)
    now = state[...] if state.shape == new_state.shape else unfold(state[...], gens)[:count]
    old = now[:horizon]
    held = now[horizon : 2 * horizon]
    duals = now[2 * horizon : 3 * horizon]
    cost = now[3 * horizon : 3 * horizon + 1]
    ceiling = now[3 * horizon + 1 : 3 * horizon + 2]
    charge_limit = bounds[0:1, :]
    start_energy = bounds[1:2, :]
    energy_limit = bounds[2:3, :]
    gen_step = jnp.clip(old - primal_step * (cost + prices[:, :gens]), 0.0, ceiling)
    gen_bar = 2.0 * gen_step - old
    gradient = efficiency * interval * running_sum(duals, True) - prices[:, gens:]
    charge_step = jnp.clip(held - primal_step * gradient, -charge_limit, charge_limit)
    charge_bar = 2.0 * charge_step - held
    bars_high, bars_low = split_halves(jnp.concatenate([gen_bar, -charge_bar], axis=1))
    bars = jnp.concatenate(
        [
            jnp.concatenate([bars_high, bars_high], axis=1),
            jnp.concatenate([bars_low, jnp.zeros_like(bars_low)], axis=1),
        ],
        axis=0,
    )
    both = matmul(bars, columns[...], rows_by_cols)
    target = held_flows[0] if order else flows
    target[...] = both[:horizon] + both[horizon:] - base_flow[...]
    if order:
        width = flows.shape[1] // len(order)
        own_far = lax.axis_index("bus") // QUAD
        for at, r in enumerate(order):
            first = pl.multiple_of((own_far ^ r) * width, width)
            flows[:, at * width : (at + 1) * width] = target[:, pl.ds(first, width)]
    energy = start_energy + efficiency * interval * running_sum(charge_bar, False)
    new_state[:horizon, :] = gen_step
    new_state[horizon : 2 * horizon, :] = charge_step
    new_state[2 * horizon : 3 * horizon, :] = clip_dual(
        duals + energy_step * energy, energy_step, 0.0, energy_limit
    )
    new_state[3 * horizon :, :] = now[3 * horizon :]


def step_units(prices, state, bounds, columns, base_flow, order=()):
    return pl.pallas_call(
        functools.partial(unit_kernel, shares=len(prices), order=order),
        in_specs=[whole_block] * (len(prices) + 4),
        out_specs=[whole_block] * 2,
        out_shape=[
            near_array((3 * base_flow.shape[0] + 2, prices[0].shape[1] // 2)),
            near_array(base_flow.shape),
        ],
        scratch_shapes=[pltpu.VMEM(base_flow.shape, jnp.float32)] if order else [],
        compiler_params=grant,
        name="step_units",
    )(*[near(a) for a in (*prices, state, bounds, columns, base_flow)])


def moved_dual(dual, limit, flows):
    return clip_dual(dual + dual_step * flows, dual_step, -limit, limit)


def line_kernel(*refs, shares):
    flows_of, (lines, columns, new_lines, prices) = refs[:shares], refs[shares:]
    horizon = prices.shape[0]
    limit = lines[horizon:, :]
    dual = moved_dual(lines[:horizon, :], limit, total(flows_of))
    new_lines[:horizon, :] = dual
    new_lines[horizon:, :] = limit
    prices[...] = local_prices(dual, columns[...])


def step_lines(flows, lines, columns):
    return pl.pallas_call(
        functools.partial(line_kernel, shares=len(flows)),
        in_specs=[whole_block] * (len(flows) + 2),
        out_specs=[whole_block] * 2,
        out_shape=[
            near_array(lines.shape),
            near_array((flows[0].shape[0], columns.shape[0] // 2)),
        ],
        compiler_params=grant,
        name="step_lines",
    )(*[near(a) for a in (*flows, lines, columns)])


def on_device(
    generation,
    charging,
    flow_dual,
    energy_dual,
    shift_factors,
    load_units,
    generator_bus,
    storage_bus,
    generator_cost,
    generator_max,
    charging_max,
    energy_init,
    energy_max,
    line_max,
    *,
    count,
):
    own_lines, horizon = flow_dual.shape
    own_units = storage_bus.shape[0]
    far = count // QUAD
    own = lax.axis_index("bus")
    member = own % QUAD
    place_of_quad = own // QUAD
    far_bits = [bit for bit in (1 << k for k in range(2, 30)) if bit < count]

    def exchange(values, bit):
        return lax.ppermute(values, "bus", [(i, i ^ bit) for i in range(count)])

    def pairs_of(bits):
        return [bits[first : first + 2] for first in range(0, len(bits), 2)]

    def hops(bits):
        if len(bits) < 2:
            return list(bits)
        low, high = bits
        return [low + high, high, low] if low < QUAD else [high, low, low + high]

    def shares(values, bits):
        for group in pairs_of(bits):
            parts = [values]
            for hop in hops(group):
                parts.append(exchange(values, hop))
            values = sum(parts)
        return parts

    alone = own_lines % 128 == 0 and len(far_bits) <= 2
    units = 2 * own_units
    scan = functools.partial(
        scan_factors, shift_factors, own_lines, far, units, horizon
    )
    other, demand_3_2, weights = scan(
        (3, 2), sources=(generator_bus[None, :], storage_bus[None, :], load_units.T)
    )
    from_y = exchange(other[units:], 2)
    from_diagonal = exchange(other[:units], 3)
    state, lines = place(
        generation.T,
        charging,
        energy_dual,
        generator_cost[None, :],
        generator_max[None, :],
        flow_dual.T,
        line_max[None, :],
        far,
        alone,
    )
    if alone:
        line_parts, line_hops = shares(lines, far_bits), [0, *hops(far_bits)]
        line_hops = [hop // QUAD for hop in line_hops]
    else:
        line_parts, line_hops = [sum(shares(lines, far_bits))], [0]
    rest, demand_0_1 = scan((0, 1), weights=weights, after=other)
    from_core = exchange(
        jnp.concatenate([rest[units:], demand_0_1[horizon:], demand_3_2[:horizon], state], axis=0),
        1,
    )
    kept = demand_0_1[:horizon] + from_core[units : units + horizon]
    sent = jnp.concatenate([demand_3_2[horizon:], state], axis=0) + from_core[units + horizon :]
    from_y_too = exchange(sent, 2)
    base_flow = kept + from_y_too[:horizon]
    state = sent[horizon:] + from_y_too[horizon:]
    bounds = lax.dynamic_slice_in_dim(
        jnp.stack([charging_max, energy_init, energy_max]),
        place_of_quad * QUAD * own_units,
        QUAD * own_units,
        axis=1,
    )

    lines, columns, prices = gather_columns(
        (rest, from_core, from_y, from_diagonal), line_parts, line_hops, horizon
    )
    for _ in range(ITERS - 1):
        state, flows = step_units(shares(prices, (1, 2)), state, bounds, columns, base_flow)
        lines, prices = step_lines(shares(flows, far_bits), lines, columns)
    mine = lambda a: lax.dynamic_slice_in_dim(a, place_of_quad * own_lines, own_lines, axis=1)
    if own_lines % 128 == 0:
        steps = len(far_bits)
        order = tuple(
            sum(((at >> k) & 1) << (steps - 1 - k) for k in range(steps)) for at in range(far)
        )
    else:
        order = ()
    state, flows = step_units(shares(prices, (1, 2)), state, bounds, columns, base_flow, order)
    if order:
        for group in pairs_of(far_bits):
            width = flows.shape[1] >> len(group)
            kept = flows[:, :width]
            for hop in hops(group):
                part = sum((hop // bit % 2) << k for k, bit in enumerate(reversed(group)))
                kept = kept + exchange(flows[:, part * width : (part + 1) * width], hop)
            flows = kept
    else:
        flows = mine(sum(shares(flows, far_bits)))
    own_dual = moved_dual(mine(lines[:horizon]), mine(lines[horizon:]), flows)
    ends = lax.dynamic_slice_in_dim(state, member * own_units, own_units, axis=1)
    return (
        ends[:horizon].T,
        ends[horizon : 2 * horizon],
        own_dual.T,
        ends[2 * horizon : 3 * horizon],
    )


def solution(mesh):
    placed = (
        P("bus", "groups"),
        P("groups", "bus"),
        P("bus", "groups"),
        P("groups", "bus"),
        P(None, "bus"),
        P("bus", "groups"),
        P("bus"),
        P("bus"),
        P("bus"),
        P("bus"),
        P(),
        P(),
        P(),
        P("bus"),
    )
    count = mesh.shape["bus"]

    def body(*args):
        return on_device(*args, count=count)

    return jax.shard_map(
        body,
        mesh=mesh,
        in_specs=placed,
        out_specs=(P("bus", "groups"), P("groups", "bus"), P("bus", "groups"), P("groups", "bus")),
        check_vma=False,
    )
```

```python
import functools

import jax
import jax.numpy as jnp
from jax import lax
from jax.experimental import pallas as pl
from jax.experimental.pallas import tpu as pltpu
from jax.sharding import PartitionSpec as P


ITERS = 3

QUAD = 4
primal_step = 0.5
dual_step = 0.5
energy_step = 0.05
efficiency = 0.95
interval = 0.125
load_unit = 0.05
rows_by_cols = (((1,), (0,)), ((), ()))
rows_by_rows = (((1,), (1,)), ((), ()))


def split_halves(values):
    high = values.astype(jnp.bfloat16)
    low = (values - high.astype(jnp.float32)).astype(jnp.bfloat16)
    return high, low


def matmul(left, right, dims):
    return lax.dot_general(left, right, dims, preferred_element_type=jnp.float32)


def clip_dual(shifted, step_size, low_bound, high_bound):
    return shifted - step_size * jnp.clip(shifted / step_size, low_bound, high_bound)


def running_sum(values, reverse):
    count = values.shape[0]
    shift = 1
    while shift < count:
        zeros = jnp.zeros((shift, values.shape[1]), values.dtype)
        if reverse:
            moved = jnp.concatenate([values[shift:], zeros], axis=0)
        else:
            moved = jnp.concatenate([zeros, values[:-shift]], axis=0)
        values = values + moved
        shift *= 2
    return values


def near_array(shape, dtype=jnp.float32):
    return pltpu.VMEM(shape, dtype)


def near(values):
    return pltpu.with_memory_space_constraint(values, pltpu.VMEM)


def far_array(values):
    return pltpu.with_memory_space_constraint(values, pltpu.HBM)


whole_block = pl.BlockSpec(memory_space=pltpu.VMEM)
grant = pltpu.CompilerParams(vmem_limit_bytes=24 << 20)


def total(refs):
    values = refs[0][...]
    for ref in refs[1:]:
        values = values + ref[...]
    return values


def as_column(row):
    width = row.shape[1]
    across = lax.broadcasted_iota(jnp.int32, (width, width), 1)
    down = lax.broadcasted_iota(jnp.int32, (width, width), 0)
    return jnp.sum(jnp.where(across == down, row, 0), axis=1, keepdims=True)


def build_weights(generator_bus, storage_bus, loads, own):
    buses = loads.shape[1]
    ids = jnp.concatenate([as_column(generator_bus), as_column(storage_bus)], axis=0)
    ids = ids - own * buses
    spots = lax.broadcasted_iota(jnp.int32, (ids.shape[0], buses), 1)
    picks = (spots == ids).astype(jnp.float32)
    rows = jnp.concatenate([picks, loads.astype(jnp.float32)], axis=0)
    return rows.astype(jnp.bfloat16)


def scan_kernel(*refs, wanted, own_lines, far, units, first_call):
    if first_call:
        generator_bus, storage_bus, loads, factors, columns, demand, weights = refs[:7]
        stage, arrived, ids_a, ids_b, counts, small = refs[7:]
    else:
        weights, factors, _, columns, demand = refs
    own = lax.axis_index("bus")
    member = own % QUAD
    few = []
    if first_call:
        for index, (source, target) in enumerate(
            ((generator_bus, ids_a), (storage_bus, ids_b), (loads, counts))
        ):
            few.append(pltpu.make_async_copy(source, target, small.at[index]))
    blocks = []
    for r in wanted:
        for z in range(far):
            first = (z * QUAD + (member ^ r)) * own_lines
            blocks.append(factors.at[pl.ds(pl.multiple_of(first, own_lines), own_lines)])
    if first_call:
        copies = [
            pltpu.make_async_copy(
                block, stage.at[pl.ds(index * own_lines, own_lines)], arrived.at[index]
            )
            for index, block in enumerate(blocks)
        ]
        for copy in few + copies[:far]:
            copy.start()
        for copy in few:
            copy.wait()
        for copy in copies[far:]:
            copy.start()
        weights[...] = build_weights(ids_a[...], ids_b[...], counts[...], own)
    rows_wanted = weights[...]
    horizon = rows_wanted.shape[0] - units
    quarter = far * own_lines
    tile = max(own_lines, min(512, quarter))
    per_tile = tile // own_lines
    for t in range(len(wanted) * quarter // tile):
        first = t * per_tile
        if first_call:
            for copy in copies[first : first + per_tile]:
                copy.wait()
            rows = stage[pl.ds(first * own_lines, tile), :]
        else:
            rows = jnp.concatenate(
                [block[...] for block in blocks[first : first + per_tile]], axis=0
            )
        high, low = split_halves(rows)
        found = matmul(rows_wanted, high, rows_by_rows) + matmul(rows_wanted, low, rows_by_rows)
        at, lane = divmod(t * tile, quarter)
        spot = pl.ds(lane, tile)
        columns[at * units : (at + 1) * units, spot] = found[:units]
        demand[at * horizon : (at + 1) * horizon, spot] = load_unit * found[units:]


def scan_factors(
    factors, own_lines, far, units, horizon, wanted, sources=(), weights=None, after=None
):
    copies = len(wanted) * far
    quarter = far * own_lines
    first_call = weights is None
    distant = pl.BlockSpec(memory_space=pltpu.HBM)
    out_shape = [
        near_array((len(wanted) * units, quarter)),
        near_array((len(wanted) * horizon, quarter)),
    ]
    scratch = []
    if first_call:
        scratch += [
            pltpu.VMEM((copies * own_lines, factors.shape[1]), jnp.float32),
            pltpu.SemaphoreType.DMA((copies,)),
        ]
        in_specs = [distant] * 4
        arrays = [far_array(a) for a in (*sources, factors)]
        out_shape.append(near_array((units + horizon, factors.shape[1]), jnp.bfloat16))
        scratch += [pltpu.VMEM(a.shape, jnp.int32) for a in sources]
        scratch.append(pltpu.SemaphoreType.DMA((3,)))
    else:
        in_specs = [whole_block, whole_block, pl.BlockSpec(memory_space=pl.ANY)]
        arrays = [near(weights), near(factors), after]
    return pl.pallas_call(
        functools.partial(
            scan_kernel,
            wanted=wanted,
            own_lines=own_lines,
            far=far,
            units=units,
            first_call=first_call,
        ),
        in_specs=in_specs,
        out_specs=[whole_block] * len(out_shape),
        out_shape=out_shape,
        scratch_shapes=scratch,
        compiler_params=grant,
        name="scan_factors",
    )(*arrays)


def fold(rows, width):
    pieces = [rows[first : first + 8, :] for first in range(0, rows.shape[0], 8)]
    per_row = width // rows.shape[1]
    while len(pieces) % per_row:
        pieces.append(jnp.zeros_like(pieces[0]))
    groups = [
        jnp.concatenate(pieces[first : first + per_row], axis=1)
        for first in range(0, len(pieces), per_row)
    ]
    return jnp.concatenate(groups, axis=0)


def unfold(folded, width):
    return jnp.concatenate(
        [
            folded[first : first + 8, lane : lane + width]
            for first in range(0, folded.shape[0], 8)
            for lane in range(0, folded.shape[1], width)
        ],
        axis=0,
    )


def place_kernel(generation, charging, energy_dual, cost, ceiling, dual, limit, state, lines):
    own = lax.axis_index("bus")

    def spread(values, repeats, slot):
        wide = jnp.concatenate([values] * repeats, axis=1)
        where = lax.broadcasted_iota(jnp.int32, wide.shape, 1) // values.shape[1]
        return jnp.where(where == slot, wide, 0.0)

    rows = [generation[...], charging[...], energy_dual[...], cost[...], ceiling[...]]
    count = sum(values.shape[0] for values in rows)
    rows.append(jnp.zeros((-count % 8, generation.shape[1]), jnp.float32))
    rows = jnp.concatenate(rows, axis=0)
    state[...] = fold(spread(rows, QUAD, own % QUAD), state.shape[1])
    own_lines = jnp.concatenate([dual[...], limit[...]], axis=0)
    if lines.shape == own_lines.shape:
        lines[...] = own_lines
    else:
        lines[...] = spread(own_lines, lines.shape[1] // own_lines.shape[1], own // QUAD)


def place(generation, charging, energy_dual, cost, ceiling, dual, limit, far, alone):
    horizon, gens = generation.shape
    quarter = far * dual.shape[1]
    pieces = (3 * horizon + 2 + 7) // 8
    per_row = quarter // (QUAD * gens)
    groups = (pieces + per_row - 1) // per_row
    return pl.pallas_call(
        place_kernel,
        out_specs=[whole_block] * 2,
        out_shape=[
            near_array((8 * groups, quarter)),
            near_array((horizon + 1, dual.shape[1] if alone else quarter)),
        ],
        compiler_params=grant,
        name="place",
    )(generation, charging, energy_dual, cost, ceiling, dual, limit)


def local_prices(dual, columns):
    horizon = dual.shape[0]
    units = columns.shape[0] // 2
    stacked = jnp.concatenate(split_halves(dual), axis=0)
    parts = matmul(stacked, columns, rows_by_rows)
    return parts[:horizon, :units] + parts[:horizon, units:] + parts[horizon:, :units]


def gather_kernel(block0, block1, block2, block3, *refs, hops):
    parts, (lines, columns, prices) = refs[:-3], refs[-3:]
    horizon = prices.shape[0]
    for hop, part in zip(hops, parts):
        if part.shape == lines.shape:
            lines[...] = part[...]
        else:
            width = part.shape[1]
            first = pl.multiple_of((lax.axis_index("bus") // QUAD ^ hop) * width, width)
            lines[:, pl.ds(first, width)] = part[...]
    units = columns.shape[0] // (2 * QUAD)
    group = units // 2
    member = lax.axis_index("bus") % QUAD
    for r, block in enumerate((block0, block1, block2, block3)):
        high, low = split_halves(block[:units, :])
        for kind in range(2):
            first = kind * QUAD * group + (member ^ r) * group
            spot = pl.ds(pl.multiple_of(first, group), group)
            columns[spot, :] = high[kind * group : (kind + 1) * group]
            first = first + QUAD * units
            spot = pl.ds(pl.multiple_of(first, group), group)
            columns[spot, :] = low[kind * group : (kind + 1) * group]
    prices[...] = local_prices(lines[:horizon, :], columns[...])


def gather_columns(blocks, parts, hops, horizon):
    units, quarter = blocks[3].shape
    arrays = [near(a) for a in (*blocks, *parts)]
    return pl.pallas_call(
        functools.partial(gather_kernel, hops=hops),
        in_specs=[whole_block] * len(arrays),
        out_specs=[whole_block] * 3,
        out_shape=[
            near_array((horizon + 1, quarter)),
            near_array((2 * QUAD * units, quarter), jnp.bfloat16),
            near_array((horizon, QUAD * units)),
        ],
        compiler_params=grant,
        name="gather_columns",
    )(*arrays)


def unit_kernel(*refs, shares, order):
    prices_of, (state, bounds, columns, base_flow, new_state, flows, *held_flows) = (
        refs[:shares],
        refs[shares:],
    )
    horizon = flows.shape[0]
    count, gens = new_state.shape
    prices = total(prices_of)
    now = state[...] if state.shape == new_state.shape else unfold(state[...], gens)[:count]
    old = now[:horizon]
    held = now[horizon : 2 * horizon]
    duals = now[2 * horizon : 3 * horizon]
    cost = now[3 * horizon : 3 * horizon + 1]
    ceiling = now[3 * horizon + 1 : 3 * horizon + 2]
    charge_limit = bounds[0:1, :]
    start_energy = bounds[1:2, :]
    energy_limit = bounds[2:3, :]
    gen_step = jnp.clip(old - primal_step * (cost + prices[:, :gens]), 0.0, ceiling)
    gen_bar = 2.0 * gen_step - old
    gradient = efficiency * interval * running_sum(duals, True) - prices[:, gens:]
    charge_step = jnp.clip(held - primal_step * gradient, -charge_limit, charge_limit)
    charge_bar = 2.0 * charge_step - held
    bars_high, bars_low = split_halves(jnp.concatenate([gen_bar, -charge_bar], axis=1))
    bars = jnp.concatenate(
        [
            jnp.concatenate([bars_high, bars_high], axis=1),
            jnp.concatenate([bars_low, jnp.zeros_like(bars_low)], axis=1),
        ],
        axis=0,
    )
    both = matmul(bars, columns[...], rows_by_cols)
    target = held_flows[0] if order else flows
    target[...] = both[:horizon] + both[horizon:] - base_flow[...]
    if order:
        width = flows.shape[1] // len(order)
        own_far = lax.axis_index("bus") // QUAD
        for at, r in enumerate(order):
            first = pl.multiple_of((own_far ^ r) * width, width)
            flows[:, at * width : (at + 1) * width] = target[:, pl.ds(first, width)]
    energy = start_energy + efficiency * interval * running_sum(charge_bar, False)
    new_state[:horizon, :] = gen_step
    new_state[horizon : 2 * horizon, :] = charge_step
    new_state[2 * horizon : 3 * horizon, :] = clip_dual(
        duals + energy_step * energy, energy_step, 0.0, energy_limit
    )
    new_state[3 * horizon :, :] = now[3 * horizon :]


def step_units(prices, state, bounds, columns, base_flow, order=()):
    return pl.pallas_call(
        functools.partial(unit_kernel, shares=len(prices), order=order),
        in_specs=[whole_block] * (len(prices) + 4),
        out_specs=[whole_block] * 2,
        out_shape=[
            near_array((3 * base_flow.shape[0] + 2, prices[0].shape[1] // 2)),
            near_array(base_flow.shape),
        ],
        scratch_shapes=[pltpu.VMEM(base_flow.shape, jnp.float32)] if order else [],
        compiler_params=grant,
        name="step_units",
    )(*[near(a) for a in (*prices, state, bounds, columns, base_flow)])


def moved_dual(dual, limit, flows):
    return clip_dual(dual + dual_step * flows, dual_step, -limit, limit)


def line_kernel(*refs, shares):
    flows_of, (lines, columns, new_lines, prices) = refs[:shares], refs[shares:]
    horizon = prices.shape[0]
    limit = lines[horizon:, :]
    dual = moved_dual(lines[:horizon, :], limit, total(flows_of))
    new_lines[:horizon, :] = dual
    new_lines[horizon:, :] = limit
    prices[...] = local_prices(dual, columns[...])


def step_lines(flows, lines, columns):
    return pl.pallas_call(
        functools.partial(line_kernel, shares=len(flows)),
        in_specs=[whole_block] * (len(flows) + 2),
        out_specs=[whole_block] * 2,
        out_shape=[
            near_array(lines.shape),
            near_array((flows[0].shape[0], columns.shape[0] // 2)),
        ],
        compiler_params=grant,
        name="step_lines",
    )(*[near(a) for a in (*flows, lines, columns)])


def on_device(
    generation,
    charging,
    flow_dual,
    energy_dual,
    shift_factors,
    load_units,
    generator_bus,
    storage_bus,
    generator_cost,
    generator_max,
    charging_max,
    energy_init,
    energy_max,
    line_max,
    *,
    count,
):
    own_lines, horizon = flow_dual.shape
    own_units = storage_bus.shape[0]
    far = count // QUAD
    own = lax.axis_index("bus")
    member = own % QUAD
    place_of_quad = own // QUAD
    far_bits = [bit for bit in (1 << k for k in range(2, 30)) if bit < count]

    def exchange(values, bit):
        return lax.ppermute(values, "bus", [(i, i ^ bit) for i in range(count)])

    def pairs_of(bits):
        return [bits[first : first + 2] for first in range(0, len(bits), 2)]

    def hops(bits):
        if len(bits) < 2:
            return list(bits)
        low, high = bits
        return [low + high, high, low] if low < QUAD else [high, low, low + high]

    def shares(values, bits, listed=()):
        for group in pairs_of(bits):
            parts = [values]
            for hop in listed or hops(group):
                parts.append(exchange(values, hop))
            values = sum(parts)
        return parts

    alone = own_lines % 128 == 0 and len(far_bits) <= 2
    units = 2 * own_units
    scan = functools.partial(
        scan_factors, shift_factors, own_lines, far, units, horizon
    )
    other, demand_3_2, weights = scan(
        (3, 2), sources=(generator_bus[None, :], storage_bus[None, :], load_units.T)
    )
    from_y = exchange(other[units:], 2)
    from_diagonal = exchange(other[:units], 3)
    state, lines = place(
        generation.T,
        charging,
        energy_dual,
        generator_cost[None, :],
        generator_max[None, :],
        flow_dual.T,
        line_max[None, :],
        far,
        alone,
    )
    if alone:
        line_parts, line_hops = shares(lines, far_bits), [0, *hops(far_bits)]
        line_hops = [hop // QUAD for hop in line_hops]
    else:
        line_parts, line_hops = [sum(shares(lines, far_bits))], [0]
    rest, demand_0_1 = scan((0, 1), weights=weights, after=other)
    from_core = exchange(
        jnp.concatenate([rest[units:], demand_0_1[horizon:], demand_3_2[:horizon], state], axis=0),
        1,
    )
    kept = demand_0_1[:horizon] + from_core[units : units + horizon]
    sent = jnp.concatenate([demand_3_2[horizon:], state], axis=0) + from_core[units + horizon :]
    from_y_too = exchange(sent, 2)
    base_flow = kept + from_y_too[:horizon]
    state = sent[horizon:] + from_y_too[horizon:]
    bounds = lax.dynamic_slice_in_dim(
        jnp.stack([charging_max, energy_init, energy_max]),
        place_of_quad * QUAD * own_units,
        QUAD * own_units,
        axis=1,
    )

    lines, columns, prices = gather_columns(
        (rest, from_core, from_y, from_diagonal), line_parts, line_hops, horizon
    )
    for iteration in range(ITERS - 1):
        state, flows = step_units(
            shares(prices, (1, 2), (2, 3, 1) if iteration == 0 else ()), state, bounds, columns, base_flow
        )
        lines, prices = step_lines(shares(flows, far_bits), lines, columns)
    mine = lambda a: lax.dynamic_slice_in_dim(a, place_of_quad * own_lines, own_lines, axis=1)
    if own_lines % 128 == 0:
        steps = len(far_bits)
        order = tuple(
            sum(((at >> k) & 1) << (steps - 1 - k) for k in range(steps)) for at in range(far)
        )
    else:
        order = ()
    state, flows = step_units(shares(prices, (1, 2)), state, bounds, columns, base_flow, order)
    if order:
        for group in pairs_of(far_bits):
            width = flows.shape[1] >> len(group)
            kept = flows[:, :width]
            for hop in hops(group):
                part = sum((hop // bit % 2) << k for k, bit in enumerate(reversed(group)))
                kept = kept + exchange(flows[:, part * width : (part + 1) * width], hop)
            flows = kept
    else:
        flows = mine(sum(shares(flows, far_bits)))
    own_dual = moved_dual(mine(lines[:horizon]), mine(lines[horizon:]), flows)
    ends = lax.dynamic_slice_in_dim(state, member * own_units, own_units, axis=1)
    return (
        ends[:horizon].T,
        ends[horizon : 2 * horizon],
        own_dual.T,
        ends[2 * horizon : 3 * horizon],
    )


def solution(mesh):
    placed = (
        P("bus", "groups"),
        P("groups", "bus"),
        P("bus", "groups"),
        P("groups", "bus"),
        P(None, "bus"),
        P("bus", "groups"),
        P("bus"),
        P("bus"),
        P("bus"),
        P("bus"),
        P(),
        P(),
        P(),
        P("bus"),
    )
    count = mesh.shape["bus"]

    def body(*args):
        return on_device(*args, count=count)

    return jax.shard_map(
        body,
        mesh=mesh,
        in_specs=placed,
        out_specs=(P("bus", "groups"), P("groups", "bus"), P("bus", "groups"), P("groups", "bus")),
        check_vma=False,
    )
```
